256 devices in a mesh: row: 8 (over x, core), col: 32 (over z, y).
Axes of the slice: x: 4, y: 4, z: 8, core: 2. Of those that a mesh axis runs over, the one named last changes fastest.
Arguments:
- region: bfloat16 [128, 1024, 256], P('row', 'col'), may hold values from -6 to 6
- reduce_weight: bfloat16 [256, 512], P(None, 'col'), may hold values from -0.375 to 0.375
- group_weight: bfloat16 [144, 512], P(None, 'col'), may hold values from -0.5 to 0.5
- expand_weight: bfloat16 [512, 512], P(None, 'col'), may hold values from -0.25 to 0.25
- shortcut_weight: bfloat16 [256, 512], P(None, 'col'), may hold values from -0.375 to 0.375
- cotangent: bfloat16 [64, 512, 512], P('row', 'col'), may hold values from -6 to 6
Outputs:
- block_out: bfloat16 [64, 512, 512], P('row', 'col')
- region_grad: bfloat16 [128, 1024, 256], P('row', 'col')
- reduce_grad: float32 [256, 512], P(None, 'col')
- group_grad: float32 [144, 512], P(None, 'col')
- expand_grad: float32 [512, 512], P(None, 'col')
- shortcut_grad: float32 [256, 512], P(None, 'col')
The draws below stay inside these ranges and needn't reach their ends.
All inputs are finite; a program needn't handle non-finite values.
Results may differ from the reference program's by a relative error of at most 0.0061.
Values may be sent and summed in bfloat16 or wider, within the bound.
A program may use at most 128 MiB of HBM per device.

```python
import jax
import jax.numpy as jnp
from jax import lax

CIN = 256
MID = 512
OUT = 512
GROUPS = 32
GW = 16
H = 128
W = 1024


def with_spikes(drawn, stream_key, source, target, parts, factor):
    def block_of(dim):
        return (jnp.arange(drawn.shape[dim]) // (drawn.shape[dim] // parts)).reshape((-1,) + (1,) * (drawn.ndim - 1 - dim))

    near = jax.random.permutation(stream_key, parts)[block_of(target)]
    second = (block_of(target) + parts // 2) % parts
    return jnp.where((block_of(source) == near) | (block_of(source) == second), factor * drawn, drawn)


def steps_of(stream_key, dims, shards, least, high):
    def one(axis_at, blocks):
        steps = jax.random.uniform(jax.random.fold_in(jax.random.fold_in(stream_key, 6), axis_at), (blocks,), jnp.float32, least / len(shards), high / len(shards))
        return jnp.repeat(jnp.exp(steps), dims[axis_at] // blocks).reshape((-1,) + (1,) * (len(dims) - axis_at - 1))

    factor_of = one(*shards[0])
    for cut in shards[1:]:
        factor_of = factor_of * one(*cut)
    return factor_of


def scatter_about(key, dims, scale, most, split=(), dtype=jnp.bfloat16):
    result = scale * jax.random.normal(key, dims, jnp.float32)
    if split:
        result = result * steps_of(key, dims, split, -0.22, 0.18)
    return jnp.clip(result, -most, most).astype(dtype)


def heavy_noise(rng, extent, deviation, most, cuts, heavy, kind=jnp.bfloat16):
    values = deviation * jax.random.normal(rng, extent, jnp.float32)
    if cuts:
        values = values * steps_of(rng, extent, cuts, -0.22, 0.18)
    return jnp.clip(with_spikes(values, jax.random.fold_in(rng, 3), *heavy), -most, most).astype(kind)


def setup_inputs(seed: int = 0) -> dict:
    seeds = jax.random.split(jax.random.key(seed), 7)
    return {
        "region": scatter_about(seeds[0], (H, W, CIN), 1.0, 6.0, ((0, 8), (1, 32))),
        "reduce_weight": scatter_about(seeds[1], (CIN, MID), CIN ** -0.5, 0.375, ((1, 32),)),
        "group_weight": scatter_about(seeds[2], (9 * GW, MID), (9 * GW) ** -0.5, 0.5, ((1, 32),)),
        "expand_weight": scatter_about(seeds[3], (MID, OUT), MID ** -0.5, 0.25, ((1, 32),)),
        "shortcut_weight": scatter_about(seeds[4], (CIN, OUT), CIN ** -0.5, 0.375, ((1, 32),)),
        "cotangent": heavy_noise(seeds[5], (H // 2, W // 2, OUT), 1.0, 6.0, ((0, 8), (1, 32)), (1, 2, 32, 2.75)),
    }


def activate(value):
    return value * jax.nn.sigmoid(value)


def slope(value):
    sigma = jax.nn.sigmoid(value)
    return sigma * (1.0 + value * (1.0 - sigma))


def reference(region, reduce_weight, group_weight, expand_weight, shortcut_weight, cotangent):
    height = region.shape[0]
    width = region.shape[1]
    rows_out = height // 2
    cols_out = width // 2
    flat = region.reshape(-1, CIN)
    pre_one = jnp.dot(flat, reduce_weight, preferred_element_type=jnp.float32).reshape(height, width, MID)
    hidden_one = activate(pre_one).astype(jnp.bfloat16)
    padded = jnp.pad(hidden_one, ((1, 0), (1, 0), (0, 0)))
    patches = []
    kernels = []
    pre_two = jnp.zeros((rows_out, cols_out, MID), jnp.float32)
    for offset in range(9):
        row_step, col_step = divmod(offset, 3)
        patch = lax.slice(padded, (row_step, col_step, 0), (row_step + height - 1, col_step + width - 1, MID), (2, 2, 1))
        patch = patch.reshape(rows_out, cols_out, GROUPS, GW).astype(jnp.float32)
        kernel = group_weight[offset * GW:(offset + 1) * GW].reshape(GW, GROUPS, GW).astype(jnp.float32)
        patches.append(patch)
        kernels.append(kernel)
        pre_two = pre_two + jnp.einsum("ijgc,cgo->ijgo", patch, kernel).reshape(rows_out, cols_out, MID)
    pre_flat = pre_two.reshape(-1, MID)
    hidden_two = activate(pre_flat).astype(jnp.bfloat16)
    strided = region[::2, ::2].reshape(-1, CIN)
    summed = jnp.dot(hidden_two, expand_weight, preferred_element_type=jnp.float32) + jnp.dot(strided, shortcut_weight, preferred_element_type=jnp.float32)
    block_out = activate(summed).astype(jnp.bfloat16).reshape(rows_out, cols_out, OUT)
    grad_sum = (cotangent.reshape(-1, OUT).astype(jnp.float32) * slope(summed)).astype(jnp.bfloat16)
    expand_grad = jnp.dot(hidden_two.T, grad_sum, preferred_element_type=jnp.float32)
    shortcut_grad = jnp.dot(strided.T, grad_sum, preferred_element_type=jnp.float32)
    grad_two = jnp.dot(grad_sum, expand_weight.T, preferred_element_type=jnp.float32)
    grad_two = (grad_two * slope(pre_flat)).astype(jnp.bfloat16)
    grad_two = grad_two.reshape(rows_out, cols_out, GROUPS, GW).astype(jnp.float32)
    spread = jnp.zeros((height + 1, width + 1, MID), jnp.float32)
    pieces = []
    for offset in range(9):
        row_step, col_step = divmod(offset, 3)
        pieces.append(jnp.einsum("ijgc,ijgo->cgo", patches[offset], grad_two).reshape(GW, MID))
        backed = jnp.einsum("ijgo,cgo->ijgc", grad_two, kernels[offset]).reshape(rows_out, cols_out, MID)
        spread = spread.at[row_step:row_step + height - 1:2, col_step:col_step + width - 1:2].add(backed)
    group_grad = jnp.concatenate(pieces, axis=0)
    grad_one = (spread[1:, 1:] * slope(pre_one)).astype(jnp.bfloat16).reshape(-1, MID)
    reduce_grad = jnp.dot(flat.T, grad_one, preferred_element_type=jnp.float32)
    region_grad = jnp.dot(grad_one, reduce_weight.T, preferred_element_type=jnp.float32).reshape(height, width, CIN)
    short_back = jnp.dot(grad_sum, shortcut_weight.T, preferred_element_type=jnp.float32).reshape(rows_out, cols_out, CIN)
    region_grad = region_grad.at[::2, ::2].add(short_back).astype(jnp.bfloat16)
    return (block_out, region_grad, reduce_grad, group_grad, expand_grad, shortcut_grad)
```

```python
import functools

import jax
import jax.numpy as jnp
from jax import lax
from jax.experimental import pallas as pl
from jax.experimental.pallas import tpu as pltpu
from jax.sharding import PartitionSpec as P

MESH = pl.DeviceIdType.MESH
BF = jnp.bfloat16
F32 = jnp.float32
NY = 4
GW = 16
LANES = 1280
HALF = LANES // 2
S = 24
PLANE = 256
MO = 224
MW = 192
PW = 48
VMEM = pl.BlockSpec(memory_space=pltpu.VMEM)

NN = (((1,), (0,)), ((), ()))
NT = (((1,), (1,)), ((), ()))


def mm(lhs, rhs, dims):
    return lax.dot_general(lhs, rhs, dims, preferred_element_type=F32)


def sigmoid(value):
    return 0.5 * jnp.tanh(0.5 * value) + 0.5


def remote(src, dst, send_sem, recv_sem, row, col):
    return pltpu.make_async_remote_copy(
        src_ref=src,
        dst_ref=dst,
        send_sem=send_sem,
        recv_sem=recv_sem,
        device_id=(row, col),
        device_id_type=MESH,
    )


def gather_kernel(
    nr, nc, wt, region, cot, full, top, bot, cbot, lft, rgt,
    reg32, cot32, lstrip, fstrip, zs, zr, ys, yr, cs, cr, hs, hr,
):
    nz = nc // NY
    row, col = lax.axis_index("row"), lax.axis_index("col")
    core = lax.rem(row, 2)
    partner = row + 1 - 2 * core
    z, y = col // NY, lax.rem(col, NY)
    lanes = pl.ds(pl.multiple_of(core * HALF, 128), HALF)

    full[z, y] = wt[...]
    for h in range(2):
        side = slice(128 * h, 128 * h + 128)
        for r in range(16):
            reg32[h, 32 * r : 32 * r + 32] = region[r, :, side].astype(F32)
        lstrip[:, side] = reg32[h, pl.ds(31, 16, stride=32), :].astype(BF)
        for q in range(2):
            fstrip[0, :, 256 * q + 128 * h : 256 * q + 128 * h + 128] = reg32[
                h, pl.ds(q, 16, stride=32), :
            ].astype(BF)
    for h in range(4):
        side = slice(128 * h, 128 * h + 128)
        for r in range(8):
            cot32[h, 16 * r : 16 * r + 16] = cot[r, :, side].astype(F32)
        first = cot32[h, pl.ds(0, 8, stride=16), :]
        fstrip[1, :, side] = jnp.concatenate([first, jnp.zeros_like(first)], axis=0).astype(BF)

    has_up, has_down = row > 0, row < nr - 1
    has_left, has_right = col > 0, col < nc - 1

    plan = [
        (has_down, 1, 0, region.at[15], top, 0),
        (has_up, -1, 0, region.at[pl.ds(0, 2)], bot, 1),
        (has_up, -1, 0, cot.at[0], cbot, 2),
    ]
    for k, (there, step) in enumerate(((has_down, 1), (None, 0), (has_up, -1))):
        right = has_right if there is None else has_right & there
        left = has_left if there is None else has_left & there
        plan.append((right, step, 1, lstrip, lft.at[k], 3 + k))
        plan.append((left, step, -1, fstrip, rgt.at[k], 6 + k))
    above = {0: has_up, 1: has_down, 2: has_down}
    for k, there in enumerate((has_up, None, has_down)):
        above[3 + k] = has_left if there is None else has_left & there
        above[6 + k] = has_right if there is None else has_right & there
    zero_of = {0: top, 1: bot, 2: cbot}
    for k in range(3):
        zero_of[3 + k] = lft.at[k]
        zero_of[6 + k] = rgt.at[k]
    for n, ref in zero_of.items():

        @pl.when(jnp.logical_not(above[n]))
        def _(ref=ref):
            ref[...] = jnp.zeros(ref.shape, ref.dtype)

    barrier = pltpu.get_barrier_semaphore()

    def greet(to_row, to_col):
        pl.semaphore_signal(barrier, inc=1, device_id=(to_row, to_col), device_id_type=MESH)

    for d in range(1, nz):
        greet(row, lax.rem(z + d, nz) * NY + y)
    for d in range(1, NY):
        greet(row, z * NY + lax.rem(y + d, NY))
    greet(partner, col)
    count = nz - 1 + NY - 1 + 1
    for dr in (-1, 0, 1):
        for dc in (-1, 0, 1):
            if dr == 0 and dc == 0:
                continue
            there = None
            for step, less, more in ((dr, has_up, has_down), (dc, has_left, has_right)):
                if step:
                    flag = more if step > 0 else less
                    there = flag if there is None else there & flag
            count = count + there.astype(jnp.int32)

            @pl.when(there)
            def _(dr=dr, dc=dc):
                greet(row + dr, col + dc)

    pl.semaphore_wait(barrier, count)

    along_z = []
    for d in range(1, nz):
        copy = remote(
            wt.at[:, lanes], full.at[z, y, :, lanes], zs.at[d], zr.at[d],
            row, lax.rem(z + d, nz) * NY + y,
        )
        copy.start()
        along_z.append(copy)
    halos = []
    for there, dr, dc, src, dst, n in plan:
        copy = remote(src, dst, hs.at[n], hr.at[n], row + dr, col + dc)
        halos.append((there, copy, n))

        @pl.when(there)
        def _(copy=copy):
            copy.start()

    for copy in along_z:
        copy.wait_recv()
    along_y = []
    for d in range(1, NY):
        copy = remote(
            full.at[:, y, :, lanes], full.at[:, y, :, lanes], ys.at[d], yr.at[d],
            row, z * NY + lax.rem(y + d, NY),
        )
        copy.start()
        along_y.append(copy)
    for copy in along_y:
        copy.wait_recv()
    across = remote(full.at[:, :, :, lanes], full.at[:, :, :, lanes], cs, cr, partner, col)
    across.start()
    for there, copy, n in halos:

        @pl.when(there)
        def _(copy=copy):
            copy.wait_send()

        @pl.when(above[n])
        def _(copy=copy):
            copy.wait_recv()

    for copy in along_z + along_y:
        copy.wait_send()
    across.wait()


def gather(nr, nc, wt, region, cot):
    nz = nc // NY
    kw = wt.shape[0]
    shape = jax.ShapeDtypeStruct
    return pl.pallas_call(
        functools.partial(gather_kernel, nr, nc),
        out_shape=(
            shape((nz, NY, kw, LANES), BF),
            shape((32, 256), BF),
            shape((2, 32, 256), BF),
            shape((16, 512), BF),
            shape((3, 16, 256), BF),
            shape((3, 2, 16, 512), BF),
        ),
        in_specs=[VMEM] * 3,
        out_specs=(VMEM,) * 6,
        scratch_shapes=[
            pltpu.VMEM((2, 512, 128), F32),
            pltpu.VMEM((4, 128, 128), F32),
            pltpu.VMEM((16, 256), BF),
            pltpu.VMEM((2, 16, 512), BF),
            pltpu.SemaphoreType.DMA((nz,)),
            pltpu.SemaphoreType.DMA((nz,)),
            pltpu.SemaphoreType.DMA((NY,)),
            pltpu.SemaphoreType.DMA((NY,)),
            pltpu.SemaphoreType.DMA,
            pltpu.SemaphoreType.DMA,
            pltpu.SemaphoreType.DMA((9,)),
            pltpu.SemaphoreType.DMA((9,)),
        ],
        compiler_params=pltpu.CompilerParams(
            collective_id=0, has_side_effects=True, vmem_limit_bytes=24 << 20
        ),
        name="gather",
    )(wt, region, cot)


def tap_source(tap):
    a, b = divmod(tap, 3)
    plane = (a % 2) * 2 + b % 2
    return plane, (a == 2) * S + (b == 2)


def block_kernel(
    region, cot, full, top, bot, cbot, lft, rgt, block_out, region_grad, gt,
    image, xp, hid, sl1, bdt, h2, sl2, c32, gs, gso, g2, gsot, g2ot, g1, g1t, rg,
):
    image[...] = jnp.zeros_like(image)
    for h in range(2):
        side = slice(128 * h, 128 * h + 128)
        for r in range(16):
            image[h, (r + 1) * PW + 1 : (r + 1) * PW + 33] = region[r, :, side].astype(F32)
        image[h, 1:33] = top[:, side].astype(F32)
        for r in range(2):
            image[h, (17 + r) * PW + 1 : (17 + r) * PW + 33] = bot[r, :, side].astype(F32)
        image[h, pl.ds(PW, 16, stride=PW), :] = lft[1, :, side].astype(F32)
        image[h, 0:1] = lft[0, :, side].astype(F32)[15:16]
        below = lft[2, :, side].astype(F32)
        for r in range(2):
            image[h, (17 + r) * PW : (17 + r) * PW + 1] = below[r : r + 1]
        for q in range(2):
            side = slice(256 * q + 128 * h, 256 * q + 128 * h + 128)
            image[h, pl.ds(PW + 33 + q, 16, stride=PW), :] = rgt[1, 0, :, side].astype(F32)
            image[h, 33 + q : 34 + q] = rgt[0, 0, :, side].astype(F32)[15:16]
            corner = rgt[2, 0, :, side].astype(F32)
            for r in range(2):
                low = (17 + r) * PW + 33 + q
                image[h, low : low + 1] = corner[r : r + 1]

    c32[...] = jnp.zeros_like(c32)
    for i in range(8):
        c32[i * S : i * S + 16] = cot[i].astype(F32)
    c32[8 * S : 8 * S + 16] = cbot[...].astype(F32)
    edge = rgt[1, 1].astype(F32)
    for i in range(8):
        c32[i * S + 16 : i * S + 17] = edge[i : i + 1]
    c32[8 * S + 16 : 8 * S + 17] = rgt[2, 1].astype(F32)[0:1]

    for k in range(4):
        pr, pc = divmod(k, 2)
        for i in range(10):
            for h in range(2):
                xp[k, i * S : (i + 1) * S, 128 * h : 128 * h + 128] = image[
                    h, pl.ds((2 * i + pr) * PW + pc, S, stride=2), :
                ]
        xp[k, 10 * S :] = jnp.zeros((PLANE - 10 * S, 256), F32)
        hid[k, 10 * S :] = jnp.zeros((PLANE - 10 * S, 512), F32)
        pixels = xp[k, : 10 * S].astype(BF)
        for n in range(2):
            half = slice(256 * n, 256 * n + 256)
            pre = mm(pixels, full[half, 0:256], NT)
            gate = sigmoid(pre)
            act = pre * gate
            hid[k, : 10 * S, half] = act.astype(BF).astype(F32)
            sl1[k, : 10 * S, half] = gate + act * (1.0 - gate)

    lane = lax.broadcasted_iota(jnp.int32, (16, 128), 1) // GW
    for tap in range(9):
        first = 1024 + 128 * (tap // 8)
        for u in range(4):
            t, v = divmod(u, 2)
            for g in range(8):
                low = u * 128 + g * 16
                piece = full[low : low + 16, first : first + 128].astype(F32)
                turn = ((g - tap % 8) * 16) % 128
                if turn:
                    piece = pltpu.roll(piece, turn, 1)
                piece = jnp.where(lane == g, piece, 0.0).astype(BF)
                low = v * 128 + g * 16
                bdt[tap, t, low : low + 16, v * 128 : v * 128 + 128] = piece
                bdt[tap, t, low : low + 16, (1 - v) * 128 : (1 - v) * 128 + 128] = jnp.zeros(
                    (16, 128), BF
                )

    for t in range(2):
        half = slice(256 * t, 256 * t + 256)
        pre = jnp.zeros((MO, 256), F32)
        for tap in range(9):
            k, off = tap_source(tap)
            pre = pre + mm(hid[k, off : off + MO, half].astype(BF), bdt[tap, t], NT)
        gate = sigmoid(pre)
        act = pre * gate
        h2[:, half] = act.astype(BF)
        sl2[:, half] = gate + act * (1.0 - gate)

    own = lax.rem(lax.broadcasted_iota(jnp.int32, (MW, 256), 0), S) < 16
    strided = xp[3, :MO].astype(BF)
    for n in range(2):
        half = slice(256 * n, 256 * n + 256)
        total = mm(h2[...], full[half, 512:1024], NT) + mm(strided, full[half, 256:512], NT)
        gate = sigmoid(total)
        act = total * gate
        for i in range(8):
            block_out[i, :, half] = act[i * S : i * S + 16].astype(BF)
        grad = c32[:, half] * (gate + act * (1.0 - gate))
        gs[:, half] = grad.astype(BF)
        kept = jnp.where(own, grad[:MW], 0.0)
        gso[:, half] = kept.astype(BF)
        gsot[half, :] = jnp.transpose(kept).astype(BF)

    for t in range(2):
        half = slice(256 * t, 256 * t + 256)
        grad = mm(gs[...], full[:, 512 + 256 * t : 768 + 256 * t], NN) * sl2[:, half]
        g2[:, half] = grad.astype(BF).astype(F32)
        g2ot[half, :] = jnp.transpose(jnp.where(own, grad[:MW], 0.0)).astype(BF)

    for n in range(2):
        half = slice(256 * n, 256 * n + 256)
        gt[half, 256:512] = mm(gsot[half, :], strided[:MW], NN).astype(BF)
        for m in range(2):
            gt[half, 512 + 256 * m : 768 + 256 * m] = mm(
                gsot[half, :], h2[:MW, 256 * m : 256 * m + 256], NN
            ).astype(BF)
    for u in range(4):
        block = slice(128 * u, 128 * u + 128)
        sums = [[jnp.zeros((16, 128), F32)] * 8, [jnp.zeros((16, 128), F32)] * 8]
        for tap in range(9):
            k, off = tap_source(tap)
            outer = mm(g2ot[block, :], hid[k, off : off + MW, block].astype(BF), NN)
            for g in range(8):
                piece = outer[g * 16 : g * 16 + 16]
                turn = ((tap % 8 - g) * 16) % 128
                if turn:
                    piece = pltpu.roll(piece, turn, 1)
                sums[tap // 8][g] = jnp.where(lane == tap % 8, piece, sums[tap // 8][g])
        for h in range(2):
            for g in range(8):
                low = u * 128 + g * 16
                gt[low : low + 16, 1024 + 128 * h : 1152 + 128 * h] = sums[h][g].astype(BF)

    for k in range(4):
        pr, pc = divmod(k, 2)
        window = (1 - pr) * S + (1 - pc)
        for t in range(2):
            half = slice(256 * t, 256 * t + 256)
            spread = jnp.zeros((MW, 256), F32)
            for tap in range(9):
                a, b = divmod(tap, 3)
                if tap_source(tap)[0] != k:
                    continue
                off = (a == 0) * S + (b == 0)
                spread = spread + mm(g2[off : off + MW, half].astype(BF), bdt[tap, t], NN)
            grad = jnp.where(own, spread * sl1[k, window : window + MW, half], 0.0)
            g1[k, :, half] = grad.astype(BF)
            g1t[k, half, :] = jnp.transpose(grad).astype(BF)
        back = mm(g1[k], full[:, 0:256], NN)
        if k == 3:
            back = back + mm(gso[...], full[:, 256:512], NN)
        for i in range(8):
            line = (2 * i + 1 - pr) * 32 + 1 - pc
            for h in range(2):
                rg[h, pl.ds(line, 16, stride=2), :] = back[
                    i * S : i * S + 16, 128 * h : 128 * h + 128
                ]
    for n in range(2):
        half = slice(256 * n, 256 * n + 256)
        grad = jnp.zeros((256, 256), F32)
        for k in range(4):
            pr, pc = divmod(k, 2)
            window = (1 - pr) * S + (1 - pc)
            grad = grad + mm(g1t[k, half, :], xp[k, window : window + MW].astype(BF), NN)
        gt[half, 0:256] = grad.astype(BF)
    for r in range(16):
        for h in range(2):
            region_grad[r, :, 128 * h : 128 * h + 128] = rg[h, 32 * r : 32 * r + 32].astype(BF)


def block(region, cot, full, *halos):
    shape = jax.ShapeDtypeStruct
    return pl.pallas_call(
        block_kernel,
        out_shape=(
            shape((8, 16, 512), BF),
            shape((16, 32, 256), BF),
            shape((512, LANES), BF),
        ),
        in_specs=[VMEM] * 8,
        out_specs=(VMEM,) * 3,
        scratch_shapes=[
            pltpu.VMEM((2, 20 * PW, 128), F32),
            pltpu.VMEM((4, PLANE, 256), F32),
            pltpu.VMEM((4, PLANE, 512), F32),
            pltpu.VMEM((4, PLANE, 512), F32),
            pltpu.VMEM((9, 2, 256, 256), BF),
            pltpu.VMEM((MO, 512), BF),
            pltpu.VMEM((MO, 512), F32),
            pltpu.VMEM((MO, 512), F32),
            pltpu.VMEM((MO, 512), BF),
            pltpu.VMEM((MW, 512), BF),
            pltpu.VMEM((MO, 512), F32),
            pltpu.VMEM((512, MW), BF),
            pltpu.VMEM((512, MW), BF),
            pltpu.VMEM((4, MW, 512), BF),
            pltpu.VMEM((4, 512, MW), BF),
            pltpu.VMEM((2, 512, 128), F32),
        ],
        compiler_params=pltpu.CompilerParams(vmem_limit_bytes=40 << 20),
        name="block",
    )(region, cot, full, *halos)


def reduce_kernel(
    nr, nc, gt, out, rc, s1, ry, s2, rz, rx,
    cs, cr, ys, yr, zs, zr, xs, xr, fs, fr,
):
    nz, nx = nc // NY, nr // 2
    row, col = lax.axis_index("row"), lax.axis_index("col")
    x, core = row // 2, lax.rem(row, 2)
    partner = row + 1 - 2 * core
    z, y = col // NY, lax.rem(col, NY)
    mine = pl.ds(pl.multiple_of(core * HALF, 128), HALF)
    other = pl.ds(pl.multiple_of((1 - core) * HALF, 128), HALF)

    barrier = pltpu.get_barrier_semaphore()

    def greet(to_row, to_col):
        pl.semaphore_signal(barrier, inc=1, device_id=(to_row, to_col), device_id_type=MESH)

    greet(partner, col)
    for d in range(1, NY):
        greet(row, z * NY + lax.rem(y + d, NY))
    for d in range(1, nz):
        greet(row, lax.rem(z + d, nz) * NY + y)
    for d in range(1, nx):
        greet(2 * lax.rem(x + d, nx) + core, col)
    pl.semaphore_wait(barrier, 1 + NY - 1 + nz - 1 + nx - 1)

    across = remote(gt.at[:, :, :, other], rc, cs, cr, partner, col)
    across.start()
    across.wait_recv()

    along_y = []
    for d in range(1, NY):
        to = lax.rem(y + d, NY)
        for n in range(nz):
            s1[n, to] = (gt[n, to, :, mine].astype(F32) + rc[n, to].astype(F32)).astype(BF)
        copy = remote(s1.at[:, to], ry.at[d], ys.at[d], yr.at[d], row, z * NY + to)
        copy.start()
        along_y.append(copy)
    for copy in along_y:
        copy.wait_recv()

    def chip_row(n):
        term = gt[n, y, :, mine].astype(F32) + rc[n, y].astype(F32)
        for d in range(1, NY):
            term = term + ry[d, n].astype(F32)
        return term

    along_z = []
    for d in range(1, nz):
        to = lax.rem(z + d, nz)
        s2[d] = chip_row(to).astype(BF)
        copy = remote(s2.at[d], rz.at[d], zs.at[d], zr.at[d], row, to * NY + y)
        copy.start()
        along_z.append(copy)
    term = chip_row(z)
    for d, copy in enumerate(along_z):
        copy.wait_recv()
        term = term + rz[d + 1].astype(F32)
    rx[x] = term

    along_x = []
    for d in range(1, nx):
        copy = remote(rx.at[x], rx.at[x], xs.at[d], xr.at[d], 2 * lax.rem(x + d, nx) + core, col)
        copy.start()
        along_x.append(copy)
    for copy in along_x:
        copy.wait_recv()
    term = rx[0]
    for n in range(1, nx):
        term = term + rx[n]
    out[:, mine] = term
    final = remote(out.at[:, mine], out.at[:, mine], fs, fr, partner, col)
    final.start()
    final.wait()
    across.wait_send()
    for copy in along_y + along_z + along_x:
        copy.wait_send()


def reduce(nr, nc, gt):
    nz, nx = nc // NY, nr // 2
    kw = gt.shape[2]
    dma = pltpu.SemaphoreType.DMA
    return pl.pallas_call(
        functools.partial(reduce_kernel, nr, nc),
        out_shape=jax.ShapeDtypeStruct((kw, LANES), F32),
        in_specs=[VMEM],
        out_specs=VMEM,
        scratch_shapes=[
            pltpu.VMEM((nz, NY, kw, HALF), BF),
            pltpu.VMEM((nz, NY, kw, HALF), BF),
            pltpu.VMEM((NY, nz, kw, HALF), BF),
            pltpu.VMEM((nz, kw, HALF), BF),
            pltpu.VMEM((nz, kw, HALF), BF),
            pltpu.VMEM((nx, kw, HALF), F32),
            dma, dma, dma((NY,)), dma((NY,)), dma((nz,)), dma((nz,)), dma((nx,)), dma((nx,)), dma, dma,
        ],
        compiler_params=pltpu.CompilerParams(
            collective_id=1, has_side_effects=True, vmem_limit_bytes=24 << 20
        ),
        name="reduce",
    )(gt)


def solution(mesh):
    nr, nc = mesh.shape["row"], mesh.shape["col"]

    def per_device(region, reduce_weight, group_weight, expand_weight, shortcut_weight, cotangent):
        kw = reduce_weight.shape[1]
        blank = jnp.zeros((LANES - 1168, kw), BF)
        wt = jnp.concatenate(
            [reduce_weight, shortcut_weight, expand_weight, group_weight, blank], axis=0
        ).T
        full, *halos = gather(nr, nc, wt, region, cotangent)
        block_out, region_grad, gt = block(region, cotangent, full.reshape(512, LANES), *halos)
        grads = reduce(nr, nc, gt.reshape(nc // NY, NY, kw, LANES)).T
        return (
            block_out, region_grad,
            grads[0:256], grads[1024:1168], grads[512:1024], grads[256:512],
        )

    weight = P(None, "col")
    tile = P("row", "col", None)
    return jax.shard_map(
        per_device,
        mesh=mesh,
        in_specs=(tile, weight, weight, weight, weight, tile),
        out_specs=(tile, tile, weight, weight, weight, weight),
        check_vma=False,
    )
```

```python
import functools

import jax
import jax.numpy as jnp
from jax import lax
from jax.experimental import pallas as pl
from jax.experimental.pallas import tpu as pltpu
from jax.sharding import PartitionSpec as P

MESH = pl.DeviceIdType.MESH
BF = jnp.bfloat16
F32 = jnp.float32
NY = 4
GW = 16
LANES = 1280
HALF = LANES // 2
S = 24
PLANE = 256
MO = 224
MW = 192
PW = 48
VMEM = pl.BlockSpec(memory_space=pltpu.VMEM)

NN = (((1,), (0,)), ((), ()))
NT = (((1,), (1,)), ((), ()))


def mm(lhs, rhs, dims):
    return lax.dot_general(lhs, rhs, dims, preferred_element_type=F32)


def sigmoid(value):
    return 0.5 * jnp.tanh(0.5 * value) + 0.5


def remote(src, dst, send_sem, recv_sem, row, col):
    return pltpu.make_async_remote_copy(
        src_ref=src,
        dst_ref=dst,
        send_sem=send_sem,
        recv_sem=recv_sem,
        device_id=(row, col),
        device_id_type=MESH,
    )


def gather_kernel(
    nr, nc, wt, region, cot, full, xp, c32,
    regv, cotv, image, lstrip, fstrip, top, bot, cbot, lft, rgt,
    ls, zs, zr, us, ur, ds, dr_, fs, fr, cs, cr, hs, hr,
):
    nz = nc // NY
    row, col = lax.axis_index("row"), lax.axis_index("col")
    core = lax.rem(row, 2)
    partner = row + 1 - 2 * core
    z, y = col // NY, lax.rem(col, NY)
    y_up, y_down, y_far = lax.rem(y + 1, NY), lax.rem(y + NY - 1, NY), lax.rem(y + 2, NY)
    lanes = pl.ds(pl.multiple_of(core * HALF, 128), HALF)
    has_up, has_down = row > 0, row < nr - 1
    has_left, has_right = col > 0, col < nc - 1

    barrier = pltpu.get_barrier_semaphore()

    def greet(to_row, to_col):
        pl.semaphore_signal(barrier, inc=1, device_id=(to_row, to_col), device_id_type=MESH)

    for d in range(1, nz):
        greet(row, lax.rem(z + d, nz) * NY + y)
    greet(row, z * NY + y_up)
    greet(row, z * NY + y_down)
    greet(partner, col)
    count = nz + 2
    for dr in (-1, 0, 1):
        for dc in (-1, 0, 1):
            if dr == 0 and dc == 0:
                continue
            there = None
            for step, less, more in ((dr, has_up, has_down), (dc, has_left, has_right)):
                if step:
                    flag = more if step > 0 else less
                    there = flag if there is None else there & flag
            count = count + there.astype(jnp.int32)

            @pl.when(there)
            def _(dr=dr, dc=dc):
                greet(row + dr, col + dc)

    loads = [
        pltpu.make_async_copy(region, regv, ls.at[0]),
        pltpu.make_async_copy(cot, cotv, ls.at[1]),
    ]
    for load in loads:
        load.start()
    full[z, y, :, lanes] = wt[:, lanes]
    image[...] = jnp.zeros_like(image)
    c32[...] = jnp.zeros_like(c32)

    plan = [
        (has_down, 1, 0, regv.at[15], top, 0),
        (has_up, -1, 0, regv.at[pl.ds(0, 2)], bot, 1),
        (has_up, -1, 0, cotv.at[0], cbot, 2),
    ]
    for k, (there, step) in enumerate(((has_down, 1), (None, 0), (has_up, -1))):
        right = has_right if there is None else has_right & there
        left = has_left if there is None else has_left & there
        plan.append((right, step, 1, lstrip, lft.at[k], 3 + k))
        plan.append((left, step, -1, fstrip, rgt.at[k], 6 + k))
    above = {0: has_up, 1: has_down, 2: has_down}
    for k, there in enumerate((has_up, None, has_down)):
        above[3 + k] = has_left if there is None else has_left & there
        above[6 + k] = has_right if there is None else has_right & there
    zero_of = {0: top, 1: bot, 2: cbot}
    for k in range(3):
        zero_of[3 + k] = lft.at[k]
        zero_of[6 + k] = rgt.at[k]
    for n, ref in zero_of.items():

        @pl.when(jnp.logical_not(above[n]))
        def _(ref=ref):
            ref[...] = jnp.zeros(ref.shape, ref.dtype)

    for load in loads:
        load.wait()
    for h in range(2):
        side = slice(128 * h, 128 * h + 128)
        for r in range(16):
            image[h, (r + 1) * PW + 1 : (r + 1) * PW + 33] = regv[r, :, side].astype(F32)
        lstrip[:, side] = image[h, pl.ds(PW + 32, 16, stride=PW), :].astype(BF)
        for q in range(2):
            fstrip[0, :, 256 * q + 128 * h : 256 * q + 128 * h + 128] = image[
                h, pl.ds(PW + 1 + q, 16, stride=PW), :
            ].astype(BF)
    for h in range(4):
        side = slice(128 * h, 128 * h + 128)
        for i in range(8):
            c32[h, i * S : i * S + 16] = cotv[i, :, side].astype(F32)
        first = c32[h, pl.ds(0, 8, stride=S), :]
        fstrip[1, :, side] = jnp.concatenate([first, jnp.zeros_like(first)], axis=0).astype(BF)

    pl.semaphore_wait(barrier, count)

    order = [1, nz - 1] if nz > 2 else [1]
    for d in range(2, nz // 2 + 1):
        order += [d, nz - d] if d < nz - d else [d]
    sent = []
    along_z = {}
    for d in order:
        copy = remote(
            wt.at[:, lanes], full.at[z, y, :, lanes], zs.at[d], zr.at[d],
            row, lax.rem(z + d, nz) * NY + y,
        )
        copy.start()
        along_z[d] = copy
    upward, downward = {}, {}

    def to_neighbours(d):
        here = full.at[lax.rem(z + nz - d, nz), y, :, lanes]
        upward[d] = remote(here, here, us.at[d], ur.at[d], row, z * NY + y_up)
        downward[d] = remote(here, here, ds.at[d], dr_.at[d], row, z * NY + y_down)
        upward[d].start()
        downward[d].start()

    to_neighbours(0)
    halos = []
    for there, dr, dc, src, dst, n in plan:
        copy = remote(src, dst, hs.at[n], hr.at[n], row + dr, col + dc)
        halos.append((there, copy, n))

        @pl.when(there)
        def _(copy=copy):
            copy.start()

    for d in order:
        along_z[d].wait_recv()
        to_neighbours(d)

    def column(at, n):
        block = full.at[:, at, :, lanes]
        copy = remote(block, block, cs.at[n], cr.at[n], partner, col)
        copy.start()
        sent.append(copy)

    column(y, 0)

    forward = {}
    for d in [0] + order:
        b = lax.rem(z + nz - d, nz)
        upward[d].wait_recv()
        if 2 * d < nz:
            here = full.at[b, y_down, :, lanes]
            forward[d] = remote(here, here, fs.at[d], fr.at[d], row, z * NY + y_up)
            forward[d].start()
        downward[d].wait_recv()
        if 2 * d >= nz:
            here = full.at[b, y_up, :, lanes]
            forward[d] = remote(here, here, fs.at[d], fr.at[d], row, z * NY + y_down)
            forward[d].start()
    column(y_up, 1)
    column(y_down, 2)

    for there, copy, n in halos:

        @pl.when(above[n])
        def _(copy=copy):
            copy.wait_recv()

    for h in range(2):
        side = slice(128 * h, 128 * h + 128)
        image[h, 1:33] = top[:, side].astype(F32)
        for r in range(2):
            image[h, (17 + r) * PW + 1 : (17 + r) * PW + 33] = bot[r, :, side].astype(F32)
        image[h, pl.ds(PW, 16, stride=PW), :] = lft[1, :, side].astype(F32)
        image[h, 0:1] = lft[0, :, side].astype(F32)[15:16]
        below = lft[2, :, side].astype(F32)
        for r in range(2):
            image[h, (17 + r) * PW : (17 + r) * PW + 1] = below[r : r + 1]
        for q in range(2):
            side = slice(256 * q + 128 * h, 256 * q + 128 * h + 128)
            image[h, pl.ds(PW + 33 + q, 16, stride=PW), :] = rgt[1, 0, :, side].astype(F32)
            image[h, 33 + q : 34 + q] = rgt[0, 0, :, side].astype(F32)[15:16]
            corner = rgt[2, 0, :, side].astype(F32)
            for r in range(2):
                low = (17 + r) * PW + 33 + q
                image[h, low : low + 1] = corner[r : r + 1]
    for h in range(4):
        side = slice(128 * h, 128 * h + 128)
        c32[h, 8 * S : 8 * S + 16] = cbot[:, side].astype(F32)
        c32[h, pl.ds(16, 8, stride=S), :] = rgt[1, 1, :, side].astype(F32)[0:8]
        c32[h, 8 * S + 16 : 8 * S + 17] = rgt[2, 1, :, side].astype(F32)[0:1]
    for k in range(4):
        pr, pc = divmod(k, 2)
        for i in range(10):
            for h in range(2):
                xp[k, i * S : (i + 1) * S, 128 * h : 128 * h + 128] = image[
                    h, pl.ds((2 * i + pr) * PW + pc, S, stride=2), :
                ]

    for d in [0] + order:
        forward[d].wait_recv()
    column(y_far, 3)
    for there, copy, n in halos:

        @pl.when(there)
        def _(copy=copy):
            copy.wait_send()

    for group in (along_z, upward, downward, forward):
        for copy in group.values():
            copy.wait_send()
    for copy in sent:
        copy.wait()


def gather(nr, nc, wt, region, cot):
    nz = nc // NY
    kw = wt.shape[0]
    shape = jax.ShapeDtypeStruct
    hbm = pl.BlockSpec(memory_space=pltpu.HBM)
    dma = pltpu.SemaphoreType.DMA
    return pl.pallas_call(
        functools.partial(gather_kernel, nr, nc),
        out_shape=(
            shape((nz, NY, kw, LANES), BF),
            shape((4, 10 * S, 256), F32),
            shape((4, MO, 128), F32),
        ),
        in_specs=[VMEM, hbm, hbm],
        out_specs=(VMEM,) * 3,
        scratch_shapes=[
            pltpu.VMEM((16, 32, 256), BF),
            pltpu.VMEM((8, 16, 512), BF),
            pltpu.VMEM((2, 20 * PW, 128), F32),
            pltpu.VMEM((16, 256), BF),
            pltpu.VMEM((2, 16, 512), BF),
            pltpu.VMEM((32, 256), BF),
            pltpu.VMEM((2, 32, 256), BF),
            pltpu.VMEM((16, 512), BF),
            pltpu.VMEM((3, 16, 256), BF),
            pltpu.VMEM((3, 2, 16, 512), BF),
            dma((2,)),
            dma((nz,)), dma((nz,)),
            dma((nz,)), dma((nz,)),
            dma((nz,)), dma((nz,)),
            dma((nz,)), dma((nz,)),
            dma((4,)), dma((4,)),
            dma((9,)), dma((9,)),
        ],
        compiler_params=pltpu.CompilerParams(
            collective_id=0, has_side_effects=True, vmem_limit_bytes=24 << 20
        ),
        name="gather",
    )(wt, region, cot)


def tap_source(tap):
    a, b = divmod(tap, 3)
    plane = (a % 2) * 2 + b % 2
    return plane, (a == 2) * S + (b == 2)


def block_kernel(
    full, xp, c32, block_out, region_grad, gt,
    hid, sl1, bdt, h2, sl2, gs, gso, g2, gsot, g2ot, g1, g1t, rg,
):
    for k in range(4):
        hid[k, 10 * S :] = jnp.zeros((PLANE - 10 * S, 512), F32)
        pixels = xp[k].astype(BF)
        for n in range(2):
            half = slice(256 * n, 256 * n + 256)
            pre = mm(pixels, full[half, 0:256], NT)
            gate = sigmoid(pre)
            act = pre * gate
            hid[k, : 10 * S, half] = act.astype(BF).astype(F32)
            sl1[k, : 10 * S, half] = gate + act * (1.0 - gate)

    lane = lax.broadcasted_iota(jnp.int32, (16, 128), 1) // GW
    for tap in range(9):
        first = 1024 + 128 * (tap // 8)
        for u in range(4):
            t, v = divmod(u, 2)
            for g in range(8):
                low = u * 128 + g * 16
                piece = full[low : low + 16, first : first + 128].astype(F32)
                turn = ((g - tap % 8) * 16) % 128
                if turn:
                    piece = pltpu.roll(piece, turn, 1)
                piece = jnp.where(lane == g, piece, 0.0).astype(BF)
                low = v * 128 + g * 16
                bdt[tap, t, low : low + 16, v * 128 : v * 128 + 128] = piece
                bdt[tap, t, low : low + 16, (1 - v) * 128 : (1 - v) * 128 + 128] = jnp.zeros(
                    (16, 128), BF
                )

    for t in range(2):
        half = slice(256 * t, 256 * t + 256)
        pre = jnp.zeros((MO, 256), F32)
        for tap in range(9):
            k, off = tap_source(tap)
            pre = pre + mm(hid[k, off : off + MO, half].astype(BF), bdt[tap, t], NT)
        gate = sigmoid(pre)
        act = pre * gate
        h2[:, half] = act.astype(BF)
        sl2[:, half] = gate + act * (1.0 - gate)

    own = lax.rem(lax.broadcasted_iota(jnp.int32, (MW, 256), 0), S) < 16
    strided = xp[3, :MO].astype(BF)
    for n in range(2):
        half = slice(256 * n, 256 * n + 256)
        total = mm(h2[...], full[half, 512:1024], NT) + mm(strided, full[half, 256:512], NT)
        gate = sigmoid(total)
        act = total * gate
        for i in range(8):
            block_out[i, :, half] = act[i * S : i * S + 16].astype(BF)
        cots = jnp.concatenate([c32[2 * n], c32[2 * n + 1]], axis=1)
        grad = cots * (gate + act * (1.0 - gate))
        gs[:, half] = grad.astype(BF)
        kept = jnp.where(own, grad[:MW], 0.0)
        gso[:, half] = kept.astype(BF)
        gsot[half, :] = jnp.transpose(kept).astype(BF)

    for t in range(2):
        half = slice(256 * t, 256 * t + 256)
        grad = mm(gs[...], full[:, 512 + 256 * t : 768 + 256 * t], NN) * sl2[:, half]
        g2[:, half] = grad.astype(BF).astype(F32)
        g2ot[half, :] = jnp.transpose(jnp.where(own, grad[:MW], 0.0)).astype(BF)

    for n in range(2):
        half = slice(256 * n, 256 * n + 256)
        gt[half, 256:512] = mm(gsot[half, :], strided[:MW], NN).astype(BF)
        for m in range(2):
            gt[half, 512 + 256 * m : 768 + 256 * m] = mm(
                gsot[half, :], h2[:MW, 256 * m : 256 * m + 256], NN
            ).astype(BF)
    for u in range(4):
        block = slice(128 * u, 128 * u + 128)
        sums = [[jnp.zeros((16, 128), F32)] * 8, [jnp.zeros((16, 128), F32)] * 8]
        for tap in range(9):
            k, off = tap_source(tap)
            outer = mm(g2ot[block, :], hid[k, off : off + MW, block].astype(BF), NN)
            for g in range(8):
                piece = outer[g * 16 : g * 16 + 16]
                turn = ((tap % 8 - g) * 16) % 128
                if turn:
                    piece = pltpu.roll(piece, turn, 1)
                sums[tap // 8][g] = jnp.where(lane == tap % 8, piece, sums[tap // 8][g])
        for h in range(2):
            for g in range(8):
                low = u * 128 + g * 16
                gt[low : low + 16, 1024 + 128 * h : 1152 + 128 * h] = sums[h][g].astype(BF)

    for k in range(4):
        pr, pc = divmod(k, 2)
        window = (1 - pr) * S + (1 - pc)
        for t in range(2):
            half = slice(256 * t, 256 * t + 256)
            spread = jnp.zeros((MW, 256), F32)
            for tap in range(9):
                a, b = divmod(tap, 3)
                if tap_source(tap)[0] != k:
                    continue
                off = (a == 0) * S + (b == 0)
                spread = spread + mm(g2[off : off + MW, half].astype(BF), bdt[tap, t], NN)
            grad = jnp.where(own, spread * sl1[k, window : window + MW, half], 0.0)
            g1[k, :, half] = grad.astype(BF)
            g1t[k, half, :] = jnp.transpose(grad).astype(BF)
        back = mm(g1[k], full[:, 0:256], NN)
        if k == 3:
            back = back + mm(gso[...], full[:, 256:512], NN)
        for i in range(8):
            line = (2 * i + 1 - pr) * 32 + 1 - pc
            for h in range(2):
                rg[h, pl.ds(line, 16, stride=2), :] = back[
                    i * S : i * S + 16, 128 * h : 128 * h + 128
                ]
    for n in range(2):
        half = slice(256 * n, 256 * n + 256)
        grad = jnp.zeros((256, 256), F32)
        for k in range(4):
            pr, pc = divmod(k, 2)
            window = (1 - pr) * S + (1 - pc)
            grad = grad + mm(g1t[k, half, :], xp[k, window : window + MW].astype(BF), NN)
        gt[half, 0:256] = grad.astype(BF)
    for r in range(16):
        for h in range(2):
            region_grad[r, :, 128 * h : 128 * h + 128] = rg[h, 32 * r : 32 * r + 32].astype(BF)


def block(full, xp, c32):
    shape = jax.ShapeDtypeStruct
    return pl.pallas_call(
        block_kernel,
        out_shape=(
            shape((8, 16, 512), BF),
            shape((16, 32, 256), BF),
            shape((512, LANES), BF),
        ),
        in_specs=[VMEM] * 3,
        out_specs=(VMEM,) * 3,
        scratch_shapes=[
            pltpu.VMEM((4, PLANE, 512), F32),
            pltpu.VMEM((4, PLANE, 512), F32),
            pltpu.VMEM((9, 2, 256, 256), BF),
            pltpu.VMEM((MO, 512), BF),
            pltpu.VMEM((MO, 512), F32),
            pltpu.VMEM((MO, 512), BF),
            pltpu.VMEM((MW, 512), BF),
            pltpu.VMEM((MO, 512), F32),
            pltpu.VMEM((512, MW), BF),
            pltpu.VMEM((512, MW), BF),
            pltpu.VMEM((4, MW, 512), BF),
            pltpu.VMEM((4, 512, MW), BF),
            pltpu.VMEM((2, 512, 128), F32),
        ],
        compiler_params=pltpu.CompilerParams(vmem_limit_bytes=40 << 20),
        name="block",
    )(full, xp, c32)


def reduce_kernel(
    nr, nc, gt, out, rc, send, land, s2, rz, rx,
    cs, cr, ys, yr, zs, zr, xs, xr, fs, fr,
):
    nz, nx = nc // NY, nr // 2
    nh = nz // 2
    row, col = lax.axis_index("row"), lax.axis_index("col")
    x, core = row // 2, lax.rem(row, 2)
    partner = row + 1 - 2 * core
    z, y = col // NY, lax.rem(col, NY)
    y_up, y_down, y_far = lax.rem(y + 1, NY), lax.rem(y + NY - 1, NY), lax.rem(y + 2, NY)
    mine = pl.ds(pl.multiple_of(core * HALF, 128), HALF)
    other = pl.ds(pl.multiple_of((1 - core) * HALF, 128), HALF)

    barrier = pltpu.get_barrier_semaphore()

    def greet(to_row, to_col):
        pl.semaphore_signal(barrier, inc=1, device_id=(to_row, to_col), device_id_type=MESH)

    greet(partner, col)
    greet(row, z * NY + y_up)
    greet(row, z * NY + y_down)
    for d in range(1, nz):
        greet(row, lax.rem(z + d, nz) * NY + y)
    for d in range(1, nx):
        greet(2 * lax.rem(x + d, nx) + core, col)
    pl.semaphore_wait(barrier, 3 + nz - 1 + nx - 1)

    across = []
    for n, at in enumerate((y_far, y_up, y_down, y)):
        copy = remote(gt.at[:, at, :, other], rc.at[:, at], cs.at[n], cr.at[n], partner, col)
        copy.start()
        across.append(copy)

    def chip(n, at):
        return gt[n, at, :, mine].astype(F32) + rc[n, at].astype(F32)

    along_y = {}

    def start_y(n, to):
        copy = remote(send.at[n], land.at[n], ys.at[n], yr.at[n], row, z * NY + to)
        copy.start()
        along_y[n] = copy

    across[0].wait_recv()
    for k in range(nh):
        send[0, k] = chip(k, y_far).astype(BF)
    start_y(0, y_up)
    for k in range(nh):
        send[1, k] = chip(nh + k, y_far).astype(BF)
    start_y(1, y_down)
    across[1].wait_recv()
    for k in range(nh):
        send[2, k] = chip(nh + k, y_up).astype(BF)
    start_y(2, y_up)
    across[2].wait_recv()
    for k in range(nh):
        send[3, k] = chip(k, y_down).astype(BF)
    start_y(3, y_down)
    along_y[0].wait_recv()
    for k in range(nh):
        send[4, k] = (chip(k, y_up) + land[0, k].astype(F32)).astype(BF)
    start_y(4, y_up)
    along_y[1].wait_recv()
    for k in range(nh):
        send[5, k] = (chip(nh + k, y_down) + land[1, k].astype(F32)).astype(BF)
    start_y(5, y_down)
    across[3].wait_recv()
    for n in (2, 3, 4, 5):
        along_y[n].wait_recv()
    for k in range(nh):
        s2[k] = chip(k, y) + land[3, k].astype(F32) + land[4, k].astype(F32)
        s2[nh + k] = chip(nh + k, y) + land[2, k].astype(F32) + land[5, k].astype(F32)

    along_z = {}
    order = [nz // 2] + [n for d in range(nz // 2 - 1, 0, -1) for n in (d, nz - d)]
    for d in order:
        to = lax.rem(z + d, nz)
        rz[0, d] = s2[to].astype(BF)
        copy = remote(rz.at[0, d], rz.at[1, d], zs.at[d], zr.at[d], row, to * NY + y)
        copy.start()
        along_z[d] = copy
    term = s2[z]
    for d in range(1, nz):
        along_z[d].wait_recv()
        term = term + rz[1, d].astype(F32)
    rx[x] = term

    along_x = []
    for d in range(1, nx):
        copy = remote(rx.at[x], rx.at[x], xs.at[d], xr.at[d], 2 * lax.rem(x + d, nx) + core, col)
        copy.start()
        along_x.append(copy)
    for copy in along_x:
        copy.wait_recv()
    term = rx[0]
    for n in range(1, nx):
        term = term + rx[n]
    out[:, mine] = term
    final = remote(out.at[:, mine], out.at[:, mine], fs, fr, partner, col)
    final.start()
    for copy in across + list(along_y.values()) + list(along_z.values()) + along_x:
        copy.wait_send()
    final.wait()


def reduce(nr, nc, gt):
    nz, nx = nc // NY, nr // 2
    kw = gt.shape[2]
    dma = pltpu.SemaphoreType.DMA
    return pl.pallas_call(
        functools.partial(reduce_kernel, nr, nc),
        out_shape=jax.ShapeDtypeStruct((kw, LANES), F32),
        in_specs=[VMEM],
        out_specs=VMEM,
        scratch_shapes=[
            pltpu.VMEM((nz, NY, kw, HALF), BF),
            pltpu.VMEM((6, nz // 2, kw, HALF), BF),
            pltpu.VMEM((6, nz // 2, kw, HALF), BF),
            pltpu.VMEM((nz, kw, HALF), F32),
            pltpu.VMEM((2, nz, kw, HALF), BF),
            pltpu.VMEM((nx, kw, HALF), F32),
            dma((4,)), dma((4,)), dma((6,)), dma((6,)), dma((nz,)), dma((nz,)), dma((nx,)), dma((nx,)), dma, dma,
        ],
        compiler_params=pltpu.CompilerParams(
            collective_id=1, has_side_effects=True, vmem_limit_bytes=24 << 20
        ),
        name="reduce",
    )(gt)


def split_kernel(slab, reduce_grad, group_grad, expand_grad, shortcut_grad):
    reduce_grad[...] = slab[:, 0:256]
    shortcut_grad[...] = slab[:, 256:512]
    expand_grad[...] = slab[:, 512:1024]
    group_grad[...] = slab[:, 1024:1168]


def split(slab):
    kw = slab.shape[0]
    return pl.pallas_call(
        split_kernel,
        out_shape=tuple(jax.ShapeDtypeStruct((kw, n), F32) for n in (256, 144, 512, 256)),
        in_specs=[VMEM],
        out_specs=(VMEM,) * 4,
        name="split",
    )(slab)


def solution(mesh):
    nr, nc = mesh.shape["row"], mesh.shape["col"]

    def per_device(region, reduce_weight, group_weight, expand_weight, shortcut_weight, cotangent):
        kw = reduce_weight.shape[1]
        blank = jnp.zeros((LANES - 1168, kw), BF)
        wt = jnp.concatenate(
            [reduce_weight, shortcut_weight, expand_weight, group_weight, blank], axis=0
        ).T
        full, xp, c32 = gather(nr, nc, wt, region, cotangent)
        block_out, region_grad, gt = block(full.reshape(512, LANES), xp, c32)
        grads = split(reduce(nr, nc, gt.reshape(nc // NY, NY, kw, LANES)))
        return (block_out, region_grad, *(grad.T for grad in grads))

    weight = P(None, "col")
    tile = P("row", "col", None)
    return jax.shard_map(
        per_device,
        mesh=mesh,
        in_specs=(tile, weight, weight, weight, weight, tile),
        out_specs=(tile, tile, weight, weight, weight, weight),
        check_vma=False,
    )
```

```python
import functools

import jax
import jax.numpy as jnp
from jax import lax
from jax.experimental import pallas as pl
from jax.experimental.pallas import tpu as pltpu
from jax.sharding import PartitionSpec as P

MESH = pl.DeviceIdType.MESH
BF = jnp.bfloat16
F32 = jnp.float32
NY = 4
GW = 16
LANES = 1280
HALF = LANES // 2
S = 24
PLANE = 256
MO = 224
MW = 192
PW = 48
VMEM = pl.BlockSpec(memory_space=pltpu.VMEM)

NN = (((1,), (0,)), ((), ()))
NT = (((1,), (1,)), ((), ()))


def mm(lhs, rhs, dims):
    return lax.dot_general(lhs, rhs, dims, preferred_element_type=F32)


def sigmoid(value):
    return 0.5 * jnp.tanh(0.5 * value) + 0.5


def remote(src, dst, send_sem, recv_sem, row, col):
    return pltpu.make_async_remote_copy(
        src_ref=src,
        dst_ref=dst,
        send_sem=send_sem,
        recv_sem=recv_sem,
        device_id=(row, col),
        device_id_type=MESH,
    )


def gather_kernel(
    nr, nc, w_reduce, w_group, w_expand, w_short, region, cot, full, xp, c32,
    wt, wg, regv, cotv, image, lstrip, fstrip, top, bot, cbot, lft, rgt,
    ls, zs, zr, us, ur, ds, dr_, fs, fr, cs, cr, hs, hr,
):
    nz = nc // NY
    row, col = lax.axis_index("row"), lax.axis_index("col")
    core = lax.rem(row, 2)
    partner = row + 1 - 2 * core
    z, y = col // NY, lax.rem(col, NY)
    y_up, y_down, y_far = lax.rem(y + 1, NY), lax.rem(y + NY - 1, NY), lax.rem(y + 2, NY)
    lanes = pl.ds(pl.multiple_of(core * HALF, 128), HALF)
    has_up, has_down = row > 0, row < nr - 1
    has_left, has_right = col > 0, col < nc - 1

    barrier = pltpu.get_barrier_semaphore()

    def greet(to_row, to_col):
        pl.semaphore_signal(barrier, inc=1, device_id=(to_row, to_col), device_id_type=MESH)

    for d in range(1, nz):
        greet(row, lax.rem(z + d, nz) * NY + y)
    greet(row, z * NY + y_up)
    greet(row, z * NY + y_down)
    greet(partner, col)
    count = nz + 2
    for dr in (-1, 0, 1):
        for dc in (-1, 0, 1):
            if dr == 0 and dc == 0:
                continue
            there = None
            for step, less, more in ((dr, has_up, has_down), (dc, has_left, has_right)):
                if step:
                    flag = more if step > 0 else less
                    there = flag if there is None else there & flag
            count = count + there.astype(jnp.int32)

            @pl.when(there)
            def _(dr=dr, dc=dc):
                greet(row + dr, col + dc)

    loads = [
        pltpu.make_async_copy(region, regv, ls.at[0]),
        pltpu.make_async_copy(cot, cotv, ls.at[1]),
        pltpu.make_async_copy(w_reduce, wt.at[:, 0:256], ls.at[2]),
        pltpu.make_async_copy(w_short, wt.at[:, 256:512], ls.at[3]),
        pltpu.make_async_copy(w_expand, wt.at[:, 512:1024], ls.at[4]),
        pltpu.make_async_copy(w_group, wg, ls.at[5]),
    ]
    for load in loads:
        load.start()
    wt[:, 1024:] = jnp.zeros_like(wt[:, 1024:])
    image[...] = jnp.zeros_like(image)
    c32[...] = jnp.zeros_like(c32)

    plan = [
        (has_down, 1, 0, regv.at[15], top, 0),
        (has_up, -1, 0, regv.at[pl.ds(0, 2)], bot, 1),
        (has_up, -1, 0, cotv.at[0], cbot, 2),
    ]
    for k, (there, step) in enumerate(((has_down, 1), (None, 0), (has_up, -1))):
        right = has_right if there is None else has_right & there
        left = has_left if there is None else has_left & there
        plan.append((right, step, 1, lstrip, lft.at[k], 3 + k))
        plan.append((left, step, -1, fstrip, rgt.at[k], 6 + k))
    above = {0: has_up, 1: has_down, 2: has_down}
    for k, there in enumerate((has_up, None, has_down)):
        above[3 + k] = has_left if there is None else has_left & there
        above[6 + k] = has_right if there is None else has_right & there
    zero_of = {0: top, 1: bot, 2: cbot}
    for k in range(3):
        zero_of[3 + k] = lft.at[k]
        zero_of[6 + k] = rgt.at[k]
    for n, ref in zero_of.items():

        @pl.when(jnp.logical_not(above[n]))
        def _(ref=ref):
            ref[...] = jnp.zeros(ref.shape, ref.dtype)

    for load in loads:
        load.wait()
    wt[:, 1024:1168] = wg[...]
    full[z, y, :, lanes] = wt[:, lanes]
    for h in range(2):
        side = slice(128 * h, 128 * h + 128)
        for r in range(16):
            image[h, (r + 1) * PW + 1 : (r + 1) * PW + 33] = regv[r, :, side].astype(F32)
        lstrip[:, side] = image[h, pl.ds(PW + 32, 16, stride=PW), :].astype(BF)
        for q in range(2):
            fstrip[0, :, 256 * q + 128 * h : 256 * q + 128 * h + 128] = image[
                h, pl.ds(PW + 1 + q, 16, stride=PW), :
            ].astype(BF)
    for h in range(4):
        side = slice(128 * h, 128 * h + 128)
        for i in range(8):
            c32[h, i * S : i * S + 16] = cotv[i, :, side].astype(F32)
        first = c32[h, pl.ds(0, 8, stride=S), :]
        fstrip[1, :, side] = jnp.concatenate([first, jnp.zeros_like(first)], axis=0).astype(BF)

    pl.semaphore_wait(barrier, count)

    order = [1, nz - 1] if nz > 2 else [1]
    for d in range(2, nz // 2 + 1):
        order += [d, nz - d] if d < nz - d else [d]
    sent = []
    along_z = {}
    for d in order:
        copy = remote(
            wt.at[:, lanes], full.at[z, y, :, lanes], zs.at[d], zr.at[d],
            row, lax.rem(z + d, nz) * NY + y,
        )
        copy.start()
        along_z[d] = copy
    upward, downward = {}, {}

    def to_neighbours(d):
        here = full.at[lax.rem(z + nz - d, nz), y, :, lanes]
        upward[d] = remote(here, here, us.at[d], ur.at[d], row, z * NY + y_up)
        downward[d] = remote(here, here, ds.at[d], dr_.at[d], row, z * NY + y_down)
        upward[d].start()
        downward[d].start()

    to_neighbours(0)
    halos = []
    for there, dr, dc, src, dst, n in plan:
        copy = remote(src, dst, hs.at[n], hr.at[n], row + dr, col + dc)
        halos.append((there, copy, n))

        @pl.when(there)
        def _(copy=copy):
            copy.start()

    for d in order:
        along_z[d].wait_recv()
        to_neighbours(d)

    def column(at, n):
        block = full.at[:, at, :, lanes]
        copy = remote(block, block, cs.at[n], cr.at[n], partner, col)
        copy.start()
        sent.append(copy)

    column(y, 0)

    forward = {}
    for d in [0] + order:
        b = lax.rem(z + nz - d, nz)
        upward[d].wait_recv()
        if 2 * d < nz:
            here = full.at[b, y_down, :, lanes]
            forward[d] = remote(here, here, fs.at[d], fr.at[d], row, z * NY + y_up)
            forward[d].start()
        downward[d].wait_recv()
        if 2 * d >= nz:
            here = full.at[b, y_up, :, lanes]
            forward[d] = remote(here, here, fs.at[d], fr.at[d], row, z * NY + y_down)
            forward[d].start()
    column(y_up, 1)
    column(y_down, 2)

    for there, copy, n in halos:

        @pl.when(above[n])
        def _(copy=copy):
            copy.wait_recv()

    for h in range(2):
        side = slice(128 * h, 128 * h + 128)
        image[h, 1:33] = top[:, side].astype(F32)
        for r in range(2):
            image[h, (17 + r) * PW + 1 : (17 + r) * PW + 33] = bot[r, :, side].astype(F32)
        image[h, pl.ds(PW, 16, stride=PW), :] = lft[1, :, side].astype(F32)
        image[h, 0:1] = lft[0, :, side].astype(F32)[15:16]
        below = lft[2, :, side].astype(F32)
        for r in range(2):
            image[h, (17 + r) * PW : (17 + r) * PW + 1] = below[r : r + 1]
        for q in range(2):
            side = slice(256 * q + 128 * h, 256 * q + 128 * h + 128)
            image[h, pl.ds(PW + 33 + q, 16, stride=PW), :] = rgt[1, 0, :, side].astype(F32)
            image[h, 33 + q : 34 + q] = rgt[0, 0, :, side].astype(F32)[15:16]
            corner = rgt[2, 0, :, side].astype(F32)
            for r in range(2):
                low = (17 + r) * PW + 33 + q
                image[h, low : low + 1] = corner[r : r + 1]
    for h in range(4):
        side = slice(128 * h, 128 * h + 128)
        c32[h, 8 * S : 8 * S + 16] = cbot[:, side].astype(F32)
        c32[h, pl.ds(16, 8, stride=S), :] = rgt[1, 1, :, side].astype(F32)[0:8]
        c32[h, 8 * S + 16 : 8 * S + 17] = rgt[2, 1, :, side].astype(F32)[0:1]
    for k in range(4):
        pr, pc = divmod(k, 2)
        for i in range(10):
            for h in range(2):
                xp[k, i * S : (i + 1) * S, 128 * h : 128 * h + 128] = image[
                    h, pl.ds((2 * i + pr) * PW + pc, S, stride=2), :
                ]

    for d in [0] + order:
        forward[d].wait_recv()
    column(y_far, 3)
    for there, copy, n in halos:

        @pl.when(there)
        def _(copy=copy):
            copy.wait_send()

    for group in (along_z, upward, downward, forward):
        for copy in group.values():
            copy.wait_send()
    for copy in sent:
        copy.wait()


def gather(nr, nc, *arrays):
    nz = nc // NY
    kw = arrays[0].shape[0]
    shape = jax.ShapeDtypeStruct
    hbm = pl.BlockSpec(memory_space=pltpu.HBM)
    dma = pltpu.SemaphoreType.DMA
    return pl.pallas_call(
        functools.partial(gather_kernel, nr, nc),
        out_shape=(
            shape((nz, NY, kw, LANES), BF),
            shape((4, 10 * S, 256), F32),
            shape((4, MO, 128), F32),
        ),
        in_specs=[hbm] * 6,
        out_specs=(VMEM,) * 3,
        scratch_shapes=[
            pltpu.VMEM((kw, LANES), BF),
            pltpu.VMEM((kw, 144), BF),
            pltpu.VMEM((16, 32, 256), BF),
            pltpu.VMEM((8, 16, 512), BF),
            pltpu.VMEM((2, 20 * PW, 128), F32),
            pltpu.VMEM((16, 256), BF),
            pltpu.VMEM((2, 16, 512), BF),
            pltpu.VMEM((32, 256), BF),
            pltpu.VMEM((2, 32, 256), BF),
            pltpu.VMEM((16, 512), BF),
            pltpu.VMEM((3, 16, 256), BF),
            pltpu.VMEM((3, 2, 16, 512), BF),
            dma((6,)),
            dma((nz,)), dma((nz,)),
            dma((nz,)), dma((nz,)),
            dma((nz,)), dma((nz,)),
            dma((nz,)), dma((nz,)),
            dma((4,)), dma((4,)),
            dma((9,)), dma((9,)),
        ],
        compiler_params=pltpu.CompilerParams(
            collective_id=0, has_side_effects=True, vmem_limit_bytes=24 << 20
        ),
        name="gather",
    )(*(pltpu.with_memory_space_constraint(a, pltpu.HBM) for a in arrays))


def tap_source(tap):
    a, b = divmod(tap, 3)
    plane = (a % 2) * 2 + b % 2
    return plane, (a == 2) * S + (b == 2)


def block_kernel(
    full, xp, c32, block_out, region_grad, hid, h2, gsot, g2ot, g1t,
    sl1, bdt, sl2, gs, gso, g2, g1, rg,
):
    for k in range(4):
        hid[k, 10 * S :] = jnp.zeros((PLANE - 10 * S, 512), F32)
        pixels = xp[k].astype(BF)
        for n in range(2):
            half = slice(256 * n, 256 * n + 256)
            pre = mm(pixels, full[half, 0:256], NT)
            gate = sigmoid(pre)
            act = pre * gate
            hid[k, : 10 * S, half] = act.astype(BF).astype(F32)
            sl1[k, : 10 * S, half] = gate + act * (1.0 - gate)

    lane = lax.broadcasted_iota(jnp.int32, (16, 128), 1) // GW
    for tap in range(9):
        first = 1024 + 128 * (tap // 8)
        for u in range(4):
            t, v = divmod(u, 2)
            for g in range(8):
                low = u * 128 + g * 16
                piece = full[low : low + 16, first : first + 128].astype(F32)
                turn = ((g - tap % 8) * 16) % 128
                if turn:
                    piece = pltpu.roll(piece, turn, 1)
                piece = jnp.where(lane == g, piece, 0.0).astype(BF)
                low = v * 128 + g * 16
                bdt[tap, t, low : low + 16, v * 128 : v * 128 + 128] = piece
                bdt[tap, t, low : low + 16, (1 - v) * 128 : (1 - v) * 128 + 128] = jnp.zeros(
                    (16, 128), BF
                )

    for t in range(2):
        half = slice(256 * t, 256 * t + 256)
        pre = jnp.zeros((MO, 256), F32)
        for tap in range(9):
            k, off = tap_source(tap)
            pre = pre + mm(hid[k, off : off + MO, half].astype(BF), bdt[tap, t], NT)
        gate = sigmoid(pre)
        act = pre * gate
        h2[:, half] = act.astype(BF)
        sl2[:, half] = gate + act * (1.0 - gate)

    own = lax.rem(lax.broadcasted_iota(jnp.int32, (MW, 256), 0), S) < 16
    strided = xp[3, :MO].astype(BF)
    for n in range(2):
        half = slice(256 * n, 256 * n + 256)
        total = mm(h2[...], full[half, 512:1024], NT) + mm(strided, full[half, 256:512], NT)
        gate = sigmoid(total)
        act = total * gate
        for i in range(8):
            block_out[i, :, half] = act[i * S : i * S + 16].astype(BF)
        cots = jnp.concatenate([c32[2 * n], c32[2 * n + 1]], axis=1)
        grad = cots * (gate + act * (1.0 - gate))
        gs[:, half] = grad.astype(BF)
        kept = jnp.where(own, grad[:MW], 0.0)
        gso[:, half] = kept.astype(BF)
        gsot[half, :] = jnp.transpose(kept).astype(BF)

    for t in range(2):
        half = slice(256 * t, 256 * t + 256)
        grad = mm(gs[...], full[:, 512 + 256 * t : 768 + 256 * t], NN) * sl2[:, half]
        g2[:, half] = grad.astype(BF).astype(F32)
        g2ot[half, :] = jnp.transpose(jnp.where(own, grad[:MW], 0.0)).astype(BF)

    for k in range(4):
        pr, pc = divmod(k, 2)
        window = (1 - pr) * S + (1 - pc)
        for t in range(2):
            half = slice(256 * t, 256 * t + 256)
            spread = jnp.zeros((MW, 256), F32)
            for tap in range(9):
                a, b = divmod(tap, 3)
                if tap_source(tap)[0] != k:
                    continue
                off = (a == 0) * S + (b == 0)
                spread = spread + mm(g2[off : off + MW, half].astype(BF), bdt[tap, t], NN)
            grad = jnp.where(own, spread * sl1[k, window : window + MW, half], 0.0)
            g1[k, :, half] = grad.astype(BF)
            g1t[k, half, :] = jnp.transpose(grad).astype(BF)
        back = mm(g1[k], full[:, 0:256], NN)
        if k == 3:
            back = back + mm(gso[...], full[:, 256:512], NN)
        for i in range(8):
            line = (2 * i + 1 - pr) * 32 + 1 - pc
            for h in range(2):
                rg[h, pl.ds(line, 16, stride=2), :] = back[
                    i * S : i * S + 16, 128 * h : 128 * h + 128
                ]
    for r in range(16):
        for h in range(2):
            region_grad[r, :, 128 * h : 128 * h + 128] = rg[h, 32 * r : 32 * r + 32].astype(BF)


def block(full, xp, c32):
    shape = jax.ShapeDtypeStruct
    return pl.pallas_call(
        block_kernel,
        out_shape=(
            shape((8, 16, 512), BF),
            shape((16, 32, 256), BF),
            shape((4, PLANE, 512), F32),
            shape((MO, 512), BF),
            shape((512, MW), BF),
            shape((512, MW), BF),
            shape((4, 512, MW), BF),
        ),
        in_specs=[VMEM] * 3,
        out_specs=(VMEM,) * 7,
        scratch_shapes=[
            pltpu.VMEM((4, PLANE, 512), F32),
            pltpu.VMEM((9, 2, 256, 256), BF),
            pltpu.VMEM((MO, 512), F32),
            pltpu.VMEM((MO, 512), BF),
            pltpu.VMEM((MW, 512), BF),
            pltpu.VMEM((MO, 512), F32),
            pltpu.VMEM((4, MW, 512), BF),
            pltpu.VMEM((2, 512, 128), F32),
        ],
        compiler_params=pltpu.CompilerParams(vmem_limit_bytes=40 << 20),
        name="block",
    )(full, xp, c32)


def weight_grads(xp, hid, h2, gsot, g2ot, g1t, gt):
    def put(first, lanes, value):
        blocks = value.reshape(value.shape[0] // (NY * GW), NY, GW, value.shape[1])
        gt[pl.ds(first // (NY * GW), blocks.shape[0]), :, :, lanes] = blocks.astype(BF)

    strided = xp[3, :MW].astype(BF)
    for n in range(2):
        half = slice(256 * n, 256 * n + 256)
        put(256 * n, slice(256, 512), mm(gsot[half, :], strided, NN))
        for m in range(2):
            cols = slice(256 * m, 256 * m + 256)
            put(256 * n, slice(512 + 256 * m, 768 + 256 * m), mm(gsot[half, :], h2[:MW, cols], NN))
        grad = jnp.zeros((256, 256), F32)
        for k in range(4):
            pr, pc = divmod(k, 2)
            window = (1 - pr) * S + (1 - pc)
            grad = grad + mm(g1t[k, half, :], xp[k, window : window + MW].astype(BF), NN)
        put(256 * n, slice(0, 256), grad)
    lane = lax.broadcasted_iota(jnp.int32, (16, 128), 1) // GW
    for u in range(4):
        block = slice(128 * u, 128 * u + 128)
        sums = [[jnp.zeros((16, 128), F32)] * 8, [jnp.zeros((16, 128), F32)] * 8]
        for tap in range(9):
            k, off = tap_source(tap)
            outer = mm(g2ot[block, :], hid[k, off : off + MW, block].astype(BF), NN)
            for g in range(8):
                piece = outer[g * 16 : g * 16 + 16]
                turn = ((tap % 8 - g) * 16) % 128
                if turn:
                    piece = pltpu.roll(piece, turn, 1)
                sums[tap // 8][g] = jnp.where(lane == tap % 8, piece, sums[tap // 8][g])
        for h in range(2):
            for g in range(8):
                at = divmod(8 * u + g, NY)
                gt[at[0], at[1], :, 1024 + 128 * h : 1152 + 128 * h] = sums[h][g].astype(BF)


def reduce_kernel(
    nr, nc, xp, hid, h2, gsot, g2ot, g1t, out, gt, rc, send, land, s2, rz, rx,
    cs, cr, ys, yr, zs, zr, xs, xr, fs, fr,
):
    nz, nx = nc // NY, nr // 2
    nh = nz // 2
    row, col = lax.axis_index("row"), lax.axis_index("col")
    x, core = row // 2, lax.rem(row, 2)
    partner = row + 1 - 2 * core
    z, y = col // NY, lax.rem(col, NY)
    y_up, y_down, y_far = lax.rem(y + 1, NY), lax.rem(y + NY - 1, NY), lax.rem(y + 2, NY)
    mine = pl.ds(pl.multiple_of(core * HALF, 128), HALF)
    other = pl.ds(pl.multiple_of((1 - core) * HALF, 128), HALF)

    barrier = pltpu.get_barrier_semaphore()

    def greet(to_row, to_col):
        pl.semaphore_signal(barrier, inc=1, device_id=(to_row, to_col), device_id_type=MESH)

    greet(partner, col)
    greet(row, z * NY + y_up)
    greet(row, z * NY + y_down)
    for d in range(1, nz):
        greet(row, lax.rem(z + d, nz) * NY + y)
    for d in range(1, nx):
        greet(2 * lax.rem(x + d, nx) + core, col)
    weight_grads(xp, hid, h2, gsot, g2ot, g1t, gt)
    pl.semaphore_wait(barrier, 3 + nz - 1 + nx - 1)

    across = []
    for n, at in enumerate((y_far, y_up, y_down, y)):
        copy = remote(gt.at[:, at, :, other], rc.at[:, at], cs.at[n], cr.at[n], partner, col)
        copy.start()
        across.append(copy)

    def chip(n, at):
        return gt[n, at, :, mine].astype(F32) + rc[n, at].astype(F32)

    along_y = {}

    def start_y(n, to):
        copy = remote(send.at[n], land.at[n], ys.at[n], yr.at[n], row, z * NY + to)
        copy.start()
        along_y[n] = copy

    across[0].wait_recv()
    for k in range(nh):
        send[0, k] = chip(k, y_far).astype(BF)
    start_y(0, y_up)
    for k in range(nh):
        send[1, k] = chip(nh + k, y_far).astype(BF)
    start_y(1, y_down)
    across[1].wait_recv()
    for k in range(nh):
        send[2, k] = chip(nh + k, y_up).astype(BF)
    start_y(2, y_up)
    across[2].wait_recv()
    for k in range(nh):
        send[3, k] = chip(k, y_down).astype(BF)
    start_y(3, y_down)
    along_y[0].wait_recv()
    for k in range(nh):
        send[4, k] = (chip(k, y_up) + land[0, k].astype(F32)).astype(BF)
    start_y(4, y_up)
    along_y[1].wait_recv()
    for k in range(nh):
        send[5, k] = (chip(nh + k, y_down) + land[1, k].astype(F32)).astype(BF)
    start_y(5, y_down)
    across[3].wait_recv()
    for n in (2, 3, 4, 5):
        along_y[n].wait_recv()
    for k in range(nh):
        s2[k] = chip(k, y) + land[3, k].astype(F32) + land[4, k].astype(F32)
        s2[nh + k] = chip(nh + k, y) + land[2, k].astype(F32) + land[5, k].astype(F32)

    along_z = {}
    order = [nz // 2] + [n for d in range(nz // 2 - 1, 0, -1) for n in (d, nz - d)]
    for d in order:
        to = lax.rem(z + d, nz)
        rz[0, d] = s2[to].astype(BF)
        copy = remote(rz.at[0, d], rz.at[1, d], zs.at[d], zr.at[d], row, to * NY + y)
        copy.start()
        along_z[d] = copy
    term = s2[z]
    for d in range(1, nz):
        along_z[d].wait_recv()
        term = term + rz[1, d].astype(F32)
    rx[x] = term

    along_x = []
    for d in range(1, nx):
        copy = remote(rx.at[x], rx.at[x], xs.at[d], xr.at[d], 2 * lax.rem(x + d, nx) + core, col)
        copy.start()
        along_x.append(copy)
    for copy in along_x:
        copy.wait_recv()
    term = rx[0]
    for n in range(1, nx):
        term = term + rx[n]
    out[:, mine] = term
    final = remote(out.at[:, mine], out.at[:, mine], fs, fr, partner, col)
    final.start()
    for copy in across + list(along_y.values()) + list(along_z.values()) + along_x:
        copy.wait_send()
    final.wait()


def reduce(nr, nc, *arrays):
    nz, nx = nc // NY, nr // 2
    kw = GW
    dma = pltpu.SemaphoreType.DMA
    return pl.pallas_call(
        functools.partial(reduce_kernel, nr, nc),
        out_shape=jax.ShapeDtypeStruct((kw, LANES), F32),
        in_specs=[VMEM] * 6,
        out_specs=VMEM,
        scratch_shapes=[
            pltpu.VMEM((nz, NY, kw, LANES), BF),
            pltpu.VMEM((nz, NY, kw, HALF), BF),
            pltpu.VMEM((6, nz // 2, kw, HALF), BF),
            pltpu.VMEM((6, nz // 2, kw, HALF), BF),
            pltpu.VMEM((nz, kw, HALF), F32),
            pltpu.VMEM((2, nz, kw, HALF), BF),
            pltpu.VMEM((nx, kw, HALF), F32),
            dma((4,)), dma((4,)), dma((6,)), dma((6,)), dma((nz,)), dma((nz,)), dma((nx,)), dma((nx,)), dma, dma,
        ],
        compiler_params=pltpu.CompilerParams(
            collective_id=1, has_side_effects=True, vmem_limit_bytes=24 << 20
        ),
        name="reduce",
    )(*arrays)


def split_kernel(slab, reduce_grad, group_grad, expand_grad, shortcut_grad, group, sems):
    copies = [
        pltpu.make_async_copy(slab.at[:, 0:256], reduce_grad, sems.at[0]),
        pltpu.make_async_copy(slab.at[:, 256:512], shortcut_grad, sems.at[1]),
        pltpu.make_async_copy(slab.at[:, 512:1024], expand_grad, sems.at[2]),
        pltpu.make_async_copy(group, group_grad, sems.at[3]),
    ]
    for copy in copies[:3]:
        copy.start()
    group[...] = slab[:, 1024:1168]
    copies[3].start()
    for copy in copies:
        copy.wait()


def split(slab):
    kw = slab.shape[0]
    return pl.pallas_call(
        split_kernel,
        out_shape=tuple(jax.ShapeDtypeStruct((kw, n), F32) for n in (256, 144, 512, 256)),
        in_specs=[VMEM],
        out_specs=(pl.BlockSpec(memory_space=pltpu.HBM),) * 4,
        scratch_shapes=[pltpu.VMEM((kw, 144), F32), pltpu.SemaphoreType.DMA((4,))],
        compiler_params=pltpu.CompilerParams(vmem_limit_bytes=2 << 20),
        name="split",
    )(slab)


def solution(mesh):
    nr, nc = mesh.shape["row"], mesh.shape["col"]

    def per_device(region, reduce_weight, group_weight, expand_weight, shortcut_weight, cotangent):
        full, xp, c32 = gather(
            nr, nc, reduce_weight.T, group_weight.T, expand_weight.T, shortcut_weight.T,
            region, cotangent,
        )
        block_out, region_grad, *terms = block(full.reshape(512, LANES), xp, c32)
        grads = split(reduce(nr, nc, xp, *terms))
        return (block_out, region_grad, *(grad.T for grad in grads))

    weight = P(None, "col")
    tile = P("row", "col", None)
    return jax.shard_map(
        per_device,
        mesh=mesh,
        in_specs=(tile, weight, weight, weight, weight, tile),
        out_specs=(tile, tile, weight, weight, weight, weight),
        check_vma=False,
    )
```

```python
import functools

import jax
import jax.numpy as jnp
from jax import lax
from jax.experimental import pallas as pl
from jax.experimental.pallas import tpu as pltpu
from jax.sharding import PartitionSpec as P

MESH = pl.DeviceIdType.MESH
BF = jnp.bfloat16
F32 = jnp.float32
NY = 4
GW = 16
LANES = 1280
HALF = LANES // 2
CHUNKS = ((0, 256), (512, 384))
LOCAL = (slice(0, 256), slice(256, 640))
S = 24
PLANE = 256
MO = 224
MW = 192
PW = 48
VMEM = pl.BlockSpec(memory_space=pltpu.VMEM)

NN = (((1,), (0,)), ((), ()))
NT = (((1,), (1,)), ((), ()))


def mm(lhs, rhs, dims):
    return lax.dot_general(lhs, rhs, dims, preferred_element_type=F32)


def sigmoid(value):
    return 0.5 * jnp.tanh(0.5 * value) + 0.5


def remote(src, dst, send_sem, recv_sem, row, col):
    return pltpu.make_async_remote_copy(
        src_ref=src,
        dst_ref=dst,
        send_sem=send_sem,
        recv_sem=recv_sem,
        device_id=(row, col),
        device_id_type=MESH,
    )


def tap_source(tap):
    a, b = divmod(tap, 3)
    plane = (a % 2) * 2 + b % 2
    return plane, (a == 2) * S + (b == 2)


def front(full, xp, hid, sl1, bdt, h2, sl2):
    weight = full[:, :, :, 0:256].reshape(512, 256)
    for k in range(4):
        hid[k, 10 * S :] = jnp.zeros((PLANE - 10 * S, 512), F32)
        pixels = xp[k].astype(BF)
        for n in range(2):
            half = slice(256 * n, 256 * n + 256)
            pre = mm(pixels, weight[half], NT)
            gate = sigmoid(pre)
            act = pre * gate
            hid[k, : 10 * S, half] = act.astype(BF).astype(F32)
            sl1[k, : 10 * S, half] = gate + act * (1.0 - gate)

    lane = lax.broadcasted_iota(jnp.int32, (16, 128), 1) // GW
    for tap in range(9):
        first = 256 + 128 * (tap // 8)
        for u in range(4):
            t, v = divmod(u, 2)
            for g in range(8):
                at = divmod(8 * u + g, NY)
                piece = full[at[0], at[1], :, first : first + 128].astype(F32)
                turn = ((g - tap % 8) * 16) % 128
                if turn:
                    piece = pltpu.roll(piece, turn, 1)
                piece = jnp.where(lane == g, piece, 0.0).astype(BF)
                low = v * 128 + g * 16
                bdt[tap, t, low : low + 16, v * 128 : v * 128 + 128] = piece
                bdt[tap, t, low : low + 16, (1 - v) * 128 : (1 - v) * 128 + 128] = jnp.zeros(
                    (16, 128), BF
                )

    for t in range(2):
        half = slice(256 * t, 256 * t + 256)
        pre = jnp.zeros((MO, 256), F32)
        for tap in range(9):
            k, off = tap_source(tap)
            pre = pre + mm(hid[k, off : off + MO, half].astype(BF), bdt[tap, t], NT)
        gate = sigmoid(pre)
        act = pre * gate
        h2[:, half] = act.astype(BF)
        sl2[:, half] = gate + act * (1.0 - gate)


def whole_kernel(
    nr, nc, w_reduce, w_group, w_expand, w_short, region, cot,
    block_out, region_grad, out,
    full, xp, c32, hid, sl1, bdt, h2, sl2, wt, wg, regv, cotv, image, lstrip, fstrip, top, bot, cbot, lft, rgt,
    gsot, g2ot, g1t, gs, gso, g2, g1, rg, gt, rc, send, land, s2, rz, rx,
    ls, zs, zr, us, ur, ds, dr_, fs, fr, cs, cr, hs, hr,
    rcs, rcr, rys, ryr, rzs, rzr, rxs, rxr, rfs, rfr,
):
    nz, nx, nh = nc // NY, nr // 2, nc // NY // 2
    row, col = lax.axis_index("row"), lax.axis_index("col")
    x, core = row // 2, lax.rem(row, 2)
    partner = row + 1 - 2 * core
    z, y = col // NY, lax.rem(col, NY)
    y_up, y_down, y_far = lax.rem(y + 1, NY), lax.rem(y + NY - 1, NY), lax.rem(y + 2, NY)
    lanes = pl.ds(pl.multiple_of(core * HALF, 128), HALF)
    has_up, has_down = row > 0, row < nr - 1
    has_left, has_right = col > 0, col < nc - 1

    barrier = pltpu.get_barrier_semaphore()

    def greet(to_row, to_col):
        pl.semaphore_signal(barrier, inc=1, device_id=(to_row, to_col), device_id_type=MESH)

    for d in range(1, nz):
        greet(row, lax.rem(z + d, nz) * NY + y)
    greet(row, z * NY + y_up)
    greet(row, z * NY + y_down)
    greet(partner, col)
    for d in range(1, nx):
        greet(2 * lax.rem(x + d, nx) + core, col)
    count = nz + 2 + nx - 1
    for dr in (-1, 0, 1):
        for dc in (-1, 0, 1):
            if dr == 0 and dc == 0:
                continue
            there = None
            for step, less, more in ((dr, has_up, has_down), (dc, has_left, has_right)):
                if step:
                    flag = more if step > 0 else less
                    there = flag if there is None else there & flag
            count = count + there.astype(jnp.int32)

            @pl.when(there)
            def _(dr=dr, dc=dc):
                greet(row + dr, col + dc)

    loads = [
        pltpu.make_async_copy(region, regv, ls.at[0]),
        pltpu.make_async_copy(cot, cotv, ls.at[1]),
        pltpu.make_async_copy(w_reduce, wt.at[:, 0:256], ls.at[2]),
        pltpu.make_async_copy(w_short, wt.at[:, 512:768], ls.at[3]),
        pltpu.make_async_copy(w_expand, wt.at[:, 768:1280], ls.at[4]),
        pltpu.make_async_copy(w_group, wg, ls.at[5]),
    ]
    for load in loads:
        load.start()
    wt[:, 256:512] = jnp.zeros((wt.shape[0], 256), BF)
    image[...] = jnp.zeros_like(image)
    c32[...] = jnp.zeros_like(c32)

    plan = [
        (has_down, 1, 0, regv.at[15], top, 0),
        (has_up, -1, 0, regv.at[pl.ds(0, 2)], bot, 1),
        (has_up, -1, 0, cotv.at[0], cbot, 2),
    ]
    for k, (there, step) in enumerate(((has_down, 1), (None, 0), (has_up, -1))):
        right = has_right if there is None else has_right & there
        left = has_left if there is None else has_left & there
        plan.append((right, step, 1, lstrip, lft.at[k], 3 + k))
        plan.append((left, step, -1, fstrip, rgt.at[k], 6 + k))
    above = {0: has_up, 1: has_down, 2: has_down}
    for k, there in enumerate((has_up, None, has_down)):
        above[3 + k] = has_left if there is None else has_left & there
        above[6 + k] = has_right if there is None else has_right & there
    zero_of = {0: top, 1: bot, 2: cbot}
    for k in range(3):
        zero_of[3 + k] = lft.at[k]
        zero_of[6 + k] = rgt.at[k]
    for n, ref in zero_of.items():

        @pl.when(jnp.logical_not(above[n]))
        def _(ref=ref):
            ref[...] = jnp.zeros(ref.shape, ref.dtype)

    for load in loads:
        load.wait()
    wt[:, 256:400] = wg[...]
    full[z, y, :, lanes] = wt[:, lanes]
    for h in range(2):
        side = slice(128 * h, 128 * h + 128)
        for r in range(16):
            image[h, (r + 1) * PW + 1 : (r + 1) * PW + 33] = regv[r, :, side].astype(F32)
        lstrip[:, side] = image[h, pl.ds(PW + 32, 16, stride=PW), :].astype(BF)
        for q in range(2):
            fstrip[0, :, 256 * q + 128 * h : 256 * q + 128 * h + 128] = image[
                h, pl.ds(PW + 1 + q, 16, stride=PW), :
            ].astype(BF)
    for h in range(4):
        side = slice(128 * h, 128 * h + 128)
        for i in range(8):
            c32[h, i * S : i * S + 16] = cotv[i, :, side].astype(F32)
        first = c32[h, pl.ds(0, 8, stride=S), :]
        fstrip[1, :, side] = jnp.concatenate([first, jnp.zeros_like(first)], axis=0).astype(BF)

    pl.semaphore_wait(barrier, count)

    order = [nz // 2] + [n for d in range(nz // 2 - 1, 0, -1) for n in (d, nz - d)]
    along_z, upward, downward, forward = {}, {}, {}, {}
    for d in order:
        copy = remote(
            wt.at[:, lanes], full.at[z, y, :, lanes], zs.at[d], zr.at[d],
            row, lax.rem(z + d, nz) * NY + y,
        )
        copy.start()
        along_z[d] = copy

    def to_neighbours(d):
        here = full.at[lax.rem(z + nz - d, nz), y, :, lanes]
        upward[d] = remote(here, here, us.at[d], ur.at[d], row, z * NY + y_up)
        downward[d] = remote(here, here, ds.at[d], dr_.at[d], row, z * NY + y_down)
        upward[d].start()
        downward[d].start()

    to_neighbours(0)
    halos = []
    for there, dr, dc, src, dst, n in plan:
        copy = remote(src, dst, hs.at[n], hr.at[n], row + dr, col + dc)
        halos.append((there, copy, n))

        @pl.when(there)
        def _(copy=copy):
            copy.start()

    nearest = [0] + order[::-1]
    for d in nearest[1:]:
        along_z[d].wait_recv()
        to_neighbours(d)

    columns = []

    def column(at):
        block = full.at[:, at, :, lanes]
        n = len(columns)
        copy = remote(block, block, cs.at[n], cr.at[n], partner, col)
        copy.start()
        columns.append(copy)

    column(y)

    for d in nearest:
        b = lax.rem(z + nz - d, nz)
        upward[d].wait_recv()
        if d % 2 == 0:
            here = full.at[b, y_down, :, lanes]
            forward[d] = remote(here, here, fs.at[d], fr.at[d], row, z * NY + y_up)
            forward[d].start()
        downward[d].wait_recv()
        if d % 2 == 1:
            here = full.at[b, y_up, :, lanes]
            forward[d] = remote(here, here, fs.at[d], fr.at[d], row, z * NY + y_down)
            forward[d].start()
    column(y_up)
    column(y_down)

    for there, copy, n in halos:

        @pl.when(above[n])
        def _(copy=copy):
            copy.wait_recv()

    for h in range(2):
        side = slice(128 * h, 128 * h + 128)
        image[h, 1:33] = top[:, side].astype(F32)
        for r in range(2):
            image[h, (17 + r) * PW + 1 : (17 + r) * PW + 33] = bot[r, :, side].astype(F32)
        image[h, pl.ds(PW, 16, stride=PW), :] = lft[1, :, side].astype(F32)
        image[h, 0:1] = lft[0, :, side].astype(F32)[15:16]
        below = lft[2, :, side].astype(F32)
        for r in range(2):
            image[h, (17 + r) * PW : (17 + r) * PW + 1] = below[r : r + 1]
        for q in range(2):
            side = slice(256 * q + 128 * h, 256 * q + 128 * h + 128)
            image[h, pl.ds(PW + 33 + q, 16, stride=PW), :] = rgt[1, 0, :, side].astype(F32)
            image[h, 33 + q : 34 + q] = rgt[0, 0, :, side].astype(F32)[15:16]
            corner = rgt[2, 0, :, side].astype(F32)
            for r in range(2):
                low = (17 + r) * PW + 33 + q
                image[h, low : low + 1] = corner[r : r + 1]
    for h in range(4):
        side = slice(128 * h, 128 * h + 128)
        c32[h, 8 * S : 8 * S + 16] = cbot[:, side].astype(F32)
        c32[h, pl.ds(16, 8, stride=S), :] = rgt[1, 1, :, side].astype(F32)[0:8]
        c32[h, 8 * S + 16 : 8 * S + 17] = rgt[2, 1, :, side].astype(F32)[0:1]
    for k in range(4):
        pr, pc = divmod(k, 2)
        for i in range(10):
            for h in range(2):
                xp[k, i * S : (i + 1) * S, 128 * h : 128 * h + 128] = image[
                    h, pl.ds((2 * i + pr) * PW + pc, S, stride=2), :
                ]

    for d in nearest:
        forward[d].wait_recv()
    column(y_far)
    for copy in columns:
        copy.wait_recv()

    front(full, xp, hid, sl1, bdt, h2, sl2)
    w_r = full[:, :, :, 0:256].reshape(512, 256)
    w_s = full[:, :, :, 512:768].reshape(512, 256)
    w_e = full[:, :, :, 768:1280].reshape(512, 512)
    mine = [pl.ds(pl.multiple_of(first + core * wide, 128), wide) for first, wide in CHUNKS]
    other = [pl.ds(pl.multiple_of(first + (1 - core) * wide, 128), wide) for first, wide in CHUNKS]
    chunks = (1, 0)

    across, along_y, turn_z, along_x, final = {}, {}, {}, {}, {}

    def start_across(q):
        for n, at in enumerate((y_far, y_up, y_down, y)):
            copy = remote(
                gt.at[:, at, :, other[q]], rc.at[:, at, :, LOCAL[q]],
                rcs.at[q, n], rcr.at[q, n], partner, col,
            )
            copy.start()
            across[q, n] = copy

    def chip(q, n, at):
        return gt[n, at, :, mine[q]].astype(F32) + rc[n, at, :, LOCAL[q]].astype(F32)

    def start_y(q, n, to):
        copy = remote(
            send.at[n, :, :, LOCAL[q]], land.at[n, :, :, LOCAL[q]],
            rys.at[q, n], ryr.at[q, n], row, z * NY + to,
        )
        copy.start()
        along_y[q, n] = copy

    def fill(q, n, low, at, extra=None):
        for k in range(nh):
            term = chip(q, low + k, at)
            if extra is not None:
                term = term + land[extra, k, :, LOCAL[q]].astype(F32)
            send[n, k, :, LOCAL[q]] = term.astype(BF)

    def y_first(q):
        across[q, 0].wait_recv()
        fill(q, 0, 0, y_far)
        start_y(q, 0, y_up)
        fill(q, 1, nh, y_far)
        start_y(q, 1, y_down)
        across[q, 1].wait_recv()
        fill(q, 2, nh, y_up)
        start_y(q, 2, y_up)
        across[q, 2].wait_recv()
        fill(q, 3, 0, y_down)
        start_y(q, 3, y_down)

    def y_second(q):
        along_y[q, 0].wait_recv()
        fill(q, 4, 0, y_up, 0)
        start_y(q, 4, y_up)
        along_y[q, 1].wait_recv()
        fill(q, 5, nh, y_down, 1)
        start_y(q, 5, y_down)

    def put(first, lanes, value):
        blocks = value.reshape(value.shape[0] // (NY * GW), NY, GW, value.shape[1])
        gt[pl.ds(first // (NY * GW), blocks.shape[0]), :, :, lanes] = blocks.astype(BF)

    own = lax.rem(lax.broadcasted_iota(jnp.int32, (MW, 256), 0), S) < 16
    strided = xp[3, :MO].astype(BF)
    for n in range(2):
        half = slice(256 * n, 256 * n + 256)
        total = mm(h2[...], w_e[half], NT) + mm(strided, w_s[half], NT)
        gate = sigmoid(total)
        act = total * gate
        for i in range(8):
            block_out[i, :, half] = act[i * S : i * S + 16].astype(BF)
        cots = jnp.concatenate([c32[2 * n], c32[2 * n + 1]], axis=1)
        grad = cots * (gate + act * (1.0 - gate))
        gs[:, half] = grad.astype(BF)
        kept = jnp.where(own, grad[:MW], 0.0)
        gso[:, half] = kept.astype(BF)
        gsot[half, :] = jnp.transpose(kept).astype(BF)

    for n in range(2):
        half = slice(256 * n, 256 * n + 256)
        put(256 * n, slice(512, 768), mm(gsot[half, :], strided[:MW], NN))
        for m in range(2):
            cols = slice(256 * m, 256 * m + 256)
            put(256 * n, slice(768 + 256 * m, 1024 + 256 * m), mm(gsot[half, :], h2[:MW, cols], NN))
    start_across(1)

    for t in range(2):
        half = slice(256 * t, 256 * t + 256)
        grad = mm(gs[...], w_e[:, 256 * t : 256 * t + 256], NN) * sl2[:, half]
        g2[:, half] = grad.astype(BF).astype(F32)
        g2ot[half, :] = jnp.transpose(jnp.where(own, grad[:MW], 0.0)).astype(BF)

    lane = lax.broadcasted_iota(jnp.int32, (16, 128), 1) // GW
    for u in range(4):
        block = slice(128 * u, 128 * u + 128)
        sums = [[jnp.zeros((16, 128), F32)] * 8, [jnp.zeros((16, 128), F32)] * 8]
        for tap in range(9):
            k, off = tap_source(tap)
            outer = mm(g2ot[block, :], hid[k, off : off + MW, block].astype(BF), NN)
            for g in range(8):
                piece = outer[g * 16 : g * 16 + 16]
                turn = ((tap % 8 - g) * 16) % 128
                if turn:
                    piece = pltpu.roll(piece, turn, 1)
                sums[tap // 8][g] = jnp.where(lane == tap % 8, piece, sums[tap // 8][g])
        for h in range(2):
            for g in range(8):
                at = divmod(8 * u + g, NY)
                gt[at[0], at[1], :, 256 + 128 * h : 384 + 128 * h] = sums[h][g].astype(BF)


    y_first(1)

    for k in range(4):
        pr, pc = divmod(k, 2)
        window = (1 - pr) * S + (1 - pc)
        for t in range(2):
            half = slice(256 * t, 256 * t + 256)
            spread = jnp.zeros((MW, 256), F32)
            for tap in range(9):
                a, b = divmod(tap, 3)
                if tap_source(tap)[0] != k:
                    continue
                off = (a == 0) * S + (b == 0)
                spread = spread + mm(g2[off : off + MW, half].astype(BF), bdt[tap, t], NN)
            grad = jnp.where(own, spread * sl1[k, window : window + MW, half], 0.0)
            g1[k, :, half] = grad.astype(BF)
            g1t[k, half, :] = jnp.transpose(grad).astype(BF)
    for n in range(2):
        half = slice(256 * n, 256 * n + 256)
        grad = jnp.zeros((256, 256), F32)
        for k in range(4):
            pr, pc = divmod(k, 2)
            window = (1 - pr) * S + (1 - pc)
            grad = grad + mm(g1t[k, half, :], xp[k, window : window + MW].astype(BF), NN)
        put(256 * n, slice(0, 256), grad)
    start_across(0)

    for k in range(4):
        pr, pc = divmod(k, 2)
        back = mm(g1[k], w_r, NN)
        if k == 3:
            back = back + mm(gso[...], w_s, NN)
        for i in range(8):
            line = (2 * i + 1 - pr) * 32 + 1 - pc
            for h in range(2):
                rg[h, pl.ds(line, 16, stride=2), :] = back[
                    i * S : i * S + 16, 128 * h : 128 * h + 128
                ]
    y_first(0)
    y_second(1)
    for r in range(16):
        for h in range(2):
            region_grad[r, :, 128 * h : 128 * h + 128] = rg[h, 32 * r : 32 * r + 32].astype(BF)
    y_second(0)

    for q in chunks:
        part = LOCAL[q]
        across[q, 3].wait_recv()
        for n in (2, 3, 4, 5):
            along_y[q, n].wait_recv()
        for k in range(nh):
            s2[k, :, part] = (
                chip(q, k, y) + land[3, k, :, part].astype(F32) + land[4, k, :, part].astype(F32)
            )
            s2[nh + k, :, part] = (
                chip(q, nh + k, y) + land[2, k, :, part].astype(F32) + land[5, k, :, part].astype(F32)
            )
        for d in order:
            to = lax.rem(z + d, nz)
            rz[0, d, :, part] = s2[to, :, part].astype(BF)
            copy = remote(
                rz.at[0, d, :, part], rz.at[1, d, :, part], rzs.at[q, d], rzr.at[q, d], row, to * NY + y
            )
            copy.start()
            turn_z[q, d] = copy
    for q in chunks:
        part = LOCAL[q]
        term = s2[z, :, part]
        for d in range(1, nz):
            turn_z[q, d].wait_recv()
            term = term + rz[1, d, :, part].astype(F32)
        rx[x, :, part] = term
        for d in range(1, nx):
            here = rx.at[x, :, part]
            copy = remote(
                here, here, rxs.at[q, d], rxr.at[q, d], 2 * lax.rem(x + d, nx) + core, col
            )
            copy.start()
            along_x[q, d] = copy
    for q in chunks:
        part = LOCAL[q]
        for d in range(1, nx):
            along_x[q, d].wait_recv()
        term = rx[0, :, part]
        for n in range(1, nx):
            term = term + rx[n, :, part]
        out[:, mine[q]] = term
        here = out.at[:, mine[q]]
        final[q] = remote(here, here, rfs.at[q], rfr.at[q], partner, col)
        final[q].start()
    for there, copy, n in halos:

        @pl.when(there)
        def _(copy=copy):
            copy.wait_send()

    for copy in columns:
        copy.wait_send()
    for group in (along_z, upward, downward, forward, across, along_y, turn_z, along_x):
        for copy in group.values():
            copy.wait_send()
    for copy in final.values():
        copy.wait()


def whole(nr, nc, *arrays):
    nz, nx = nc // NY, nr // 2
    kw = GW
    shape = jax.ShapeDtypeStruct
    hbm = pl.BlockSpec(memory_space=pltpu.HBM)
    dma = pltpu.SemaphoreType.DMA
    return pl.pallas_call(
        functools.partial(whole_kernel, nr, nc),
        out_shape=(
            shape((8, 16, 512), BF),
            shape((16, 32, 256), BF),
            shape((kw, LANES), F32),
        ),
        in_specs=[hbm] * 6,
        out_specs=(VMEM,) * 3,
        scratch_shapes=[
            pltpu.VMEM((nz, NY, kw, LANES), BF),
            pltpu.VMEM((4, 10 * S, 256), F32),
            pltpu.VMEM((4, MO, 128), F32),
            pltpu.VMEM((4, PLANE, 512), F32),
            pltpu.VMEM((4, PLANE, 512), F32),
            pltpu.VMEM((9, 2, 256, 256), BF),
            pltpu.VMEM((MO, 512), BF),
            pltpu.VMEM((MO, 512), F32),
            pltpu.VMEM((kw, LANES), BF),
            pltpu.VMEM((kw, 144), BF),
            pltpu.VMEM((16, 32, 256), BF),
            pltpu.VMEM((8, 16, 512), BF),
            pltpu.VMEM((2, 20 * PW, 128), F32),
            pltpu.VMEM((16, 256), BF),
            pltpu.VMEM((2, 16, 512), BF),
            pltpu.VMEM((32, 256), BF),
            pltpu.VMEM((2, 32, 256), BF),
            pltpu.VMEM((16, 512), BF),
            pltpu.VMEM((3, 16, 256), BF),
            pltpu.VMEM((3, 2, 16, 512), BF),
            pltpu.VMEM((512, MW), BF),
            pltpu.VMEM((512, MW), BF),
            pltpu.VMEM((4, 512, MW), BF),
            pltpu.VMEM((MO, 512), BF),
            pltpu.VMEM((MW, 512), BF),
            pltpu.VMEM((MO, 512), F32),
            pltpu.VMEM((4, MW, 512), BF),
            pltpu.VMEM((2, 512, 128), F32),
            pltpu.VMEM((nz, NY, kw, LANES), BF),
            pltpu.VMEM((nz, NY, kw, HALF), BF),
            pltpu.VMEM((6, nz // 2, kw, HALF), BF),
            pltpu.VMEM((6, nz // 2, kw, HALF), BF),
            pltpu.VMEM((nz, kw, HALF), F32),
            pltpu.VMEM((2, nz, kw, HALF), BF),
            pltpu.VMEM((nx, kw, HALF), F32),
            dma((6,)),
            dma((nz,)), dma((nz,)), dma((nz,)), dma((nz,)),
            dma((nz,)), dma((nz,)), dma((nz,)), dma((nz,)),
            dma((4,)), dma((4,)), dma((9,)), dma((9,)),
            dma((2, 4)), dma((2, 4)), dma((2, 6)), dma((2, 6)),
            dma((2, nz)), dma((2, nz)), dma((2, nx)), dma((2, nx)), dma((2,)), dma((2,)),
        ],
        compiler_params=pltpu.CompilerParams(
            collective_id=0, has_side_effects=True, vmem_limit_bytes=48 << 20
        ),
        name="whole",
    )(*(pltpu.with_memory_space_constraint(a, pltpu.HBM) for a in arrays))


def store_kernel(
    block_out, region_grad, slab,
    block_to, region_to, reduce_grad, group_grad, expand_grad, shortcut_grad, group, sems,
):
    pairs = [
        (region_grad, region_to),
        (block_out, block_to),
        (slab.at[:, 768:1280], expand_grad),
        (slab.at[:, 0:256], reduce_grad),
        (slab.at[:, 512:768], shortcut_grad),
        (group, group_grad),
    ]
    copies = [pltpu.make_async_copy(a, b, sems.at[n]) for n, (a, b) in enumerate(pairs)]
    for copy in copies[:-1]:
        copy.start()
    group[...] = slab[:, 256:400]
    copies[-1].start()
    for copy in copies:
        copy.wait()


def store(block_out, region_grad, slab):
    kw = slab.shape[0]
    shape = jax.ShapeDtypeStruct
    return pl.pallas_call(
        store_kernel,
        out_shape=(
            shape(block_out.shape, BF),
            shape(region_grad.shape, BF),
            *(shape((kw, n), F32) for n in (256, 144, 512, 256)),
        ),
        in_specs=[VMEM] * 3,
        out_specs=(pl.BlockSpec(memory_space=pltpu.HBM),) * 6,
        scratch_shapes=[pltpu.VMEM((kw, 144), F32), pltpu.SemaphoreType.DMA((6,))],
        compiler_params=pltpu.CompilerParams(vmem_limit_bytes=4 << 20),
        name="store",
    )(block_out, region_grad, slab)


def solution(mesh):
    nr, nc = mesh.shape["row"], mesh.shape["col"]

    def per_device(region, reduce_weight, group_weight, expand_weight, shortcut_weight, cotangent):
        block_out, region_grad, *grads = store(
            *whole(
                nr, nc, reduce_weight.T, group_weight.T, expand_weight.T, shortcut_weight.T,
                region, cotangent,
            )
        )
        return (block_out, region_grad, *(grad.T for grad in grads))

    weight = P(None, "col")
    tile = P("row", "col", None)
    return jax.shard_map(
        per_device,
        mesh=mesh,
        in_specs=(tile, weight, weight, weight, weight, tile),
        out_specs=(tile, tile, weight, weight, weight, weight),
        check_vma=False,
    )
```

```python
import functools

import jax
import jax.numpy as jnp
from jax import lax
from jax.experimental import pallas as pl
from jax.experimental.pallas import tpu as pltpu
from jax.sharding import PartitionSpec as P

MESH = pl.DeviceIdType.MESH
BF = jnp.bfloat16
F32 = jnp.float32
NY = 4
GW = 16
LANES = 1280
HALF = LANES // 2
CHUNKS = ((0, 256), (512, 384))
LOCAL = (slice(0, 256), slice(256, 640))
S = 24
PLANE = 256
MO = 224
MW = 192
PW = 48
VMEM = pl.BlockSpec(memory_space=pltpu.VMEM)

NN = (((1,), (0,)), ((), ()))
NT = (((1,), (1,)), ((), ()))


def mm(lhs, rhs, dims):
    return lax.dot_general(lhs, rhs, dims, preferred_element_type=F32)


def sigmoid(value):
    return 0.5 * jnp.tanh(0.5 * value) + 0.5


def remote(src, dst, send_sem, recv_sem, row, col):
    return pltpu.make_async_remote_copy(
        src_ref=src,
        dst_ref=dst,
        send_sem=send_sem,
        recv_sem=recv_sem,
        device_id=(row, col),
        device_id_type=MESH,
    )


def tap_source(tap):
    a, b = divmod(tap, 3)
    plane = (a % 2) * 2 + b % 2
    return plane, (a == 2) * S + (b == 2)


def front(full, xp, hid, sl1, bdt, h2, sl2):
    weight = full[:, :, :, 0:256].reshape(512, 256)
    for k in range(4):
        hid[k, 10 * S :] = jnp.zeros((PLANE - 10 * S, 512), F32)
        pixels = xp[k].astype(BF)
        for n in range(2):
            half = slice(256 * n, 256 * n + 256)
            pre = mm(pixels, weight[half], NT)
            gate = sigmoid(pre)
            act = pre * gate
            hid[k, : 10 * S, half] = act.astype(BF).astype(F32)
            sl1[k, : 10 * S, half] = gate + act * (1.0 - gate)

    lane = lax.broadcasted_iota(jnp.int32, (16, 128), 1) // GW
    for tap in range(9):
        first = 256 + 128 * (tap // 8)
        for u in range(4):
            t, v = divmod(u, 2)
            for g in range(8):
                at = divmod(8 * u + g, NY)
                piece = full[at[0], at[1], :, first : first + 128].astype(F32)
                turn = ((g - tap % 8) * 16) % 128
                if turn:
                    piece = pltpu.roll(piece, turn, 1)
                piece = jnp.where(lane == g, piece, 0.0).astype(BF)
                low = v * 128 + g * 16
                bdt[tap, t, low : low + 16, v * 128 : v * 128 + 128] = piece
                bdt[tap, t, low : low + 16, (1 - v) * 128 : (1 - v) * 128 + 128] = jnp.zeros(
                    (16, 128), BF
                )

    for t in range(2):
        half = slice(256 * t, 256 * t + 256)
        pre = jnp.zeros((MO, 256), F32)
        for tap in range(9):
            k, off = tap_source(tap)
            pre = pre + mm(hid[k, off : off + MO, half].astype(BF), bdt[tap, t], NT)
        gate = sigmoid(pre)
        act = pre * gate
        h2[:, half] = act.astype(BF)
        sl2[:, half] = gate + act * (1.0 - gate)


def whole_kernel(
    nr, nc, w_reduce, w_group, w_expand, w_short, region, cot,
    block_out, region_grad, out,
    full, xp, c32, hid, sl1, bdt, h2, sl2, wt, wg, regv, cotv, image, lstrip, fstrip, top, bot, cbot, lft, rgt,
    gsot, g2ot, g1t, gs, gso, g2, g1, rg, gt, rc, send, land, s2, rz, rx,
    ls, zs, zr, us, ur, ds, dr_, fs, fr, cs, cr, hs, hr,
    rcs, rcr, rys, ryr, rzs, rzr, rxs, rxr,
):
    nz, nx, nh = nc // NY, nr // 2, nc // NY // 2
    row, col = lax.axis_index("row"), lax.axis_index("col")
    x, core = row // 2, lax.rem(row, 2)
    partner = row + 1 - 2 * core
    z, y = col // NY, lax.rem(col, NY)
    y_up, y_down, y_far = lax.rem(y + 1, NY), lax.rem(y + NY - 1, NY), lax.rem(y + 2, NY)
    lanes = pl.ds(pl.multiple_of(core * HALF, 128), HALF)
    has_up, has_down = row > 0, row < nr - 1
    has_left, has_right = col > 0, col < nc - 1

    barrier = pltpu.get_barrier_semaphore()

    def greet(to_row, to_col):
        pl.semaphore_signal(barrier, inc=1, device_id=(to_row, to_col), device_id_type=MESH)

    for d in range(1, nz):
        greet(row, lax.rem(z + d, nz) * NY + y)
    greet(row, z * NY + y_up)
    greet(row, z * NY + y_down)
    greet(row, z * NY + y_far)
    greet(partner, col)
    for d in range(1, nx):
        greet(2 * lax.rem(x + d, nx), col)
        greet(2 * lax.rem(x + d, nx) + 1, col)
    count = nz + 3 + 2 * (nx - 1)
    for dr in (-1, 0, 1):
        for dc in (-1, 0, 1):
            if dr == 0 and dc == 0:
                continue
            there = None
            for step, less, more in ((dr, has_up, has_down), (dc, has_left, has_right)):
                if step:
                    flag = more if step > 0 else less
                    there = flag if there is None else there & flag
            count = count + there.astype(jnp.int32)

            @pl.when(there)
            def _(dr=dr, dc=dc):
                greet(row + dr, col + dc)

    loads = [
        pltpu.make_async_copy(region, regv, ls.at[0]),
        pltpu.make_async_copy(cot, cotv, ls.at[1]),
        pltpu.make_async_copy(w_reduce, wt.at[:, 0:256], ls.at[2]),
        pltpu.make_async_copy(w_short, wt.at[:, 512:768], ls.at[3]),
        pltpu.make_async_copy(w_expand, wt.at[:, 768:1280], ls.at[4]),
        pltpu.make_async_copy(w_group, wg, ls.at[5]),
    ]
    for load in loads:
        load.start()
    wt[:, 256:512] = jnp.zeros((wt.shape[0], 256), BF)
    image[...] = jnp.zeros_like(image)
    c32[...] = jnp.zeros_like(c32)

    lpart = (pl.ds(8, 8), pl.ds(0, 16), pl.ds(0, 8))
    fpart = (pl.ds(0, 1), pl.ds(0, 3), pl.ds(1, 2))
    plan = [
        (has_down, 1, 0, regv.at[15], top, 0),
        (has_up, -1, 0, regv.at[pl.ds(0, 2)], bot, 1),
        (has_up, -1, 0, cotv.at[0], cbot, 2),
    ]
    for k, (there, step) in enumerate(((has_down, 1), (None, 0), (has_up, -1))):
        right = has_right if there is None else has_right & there
        left = has_left if there is None else has_left & there
        plan.append((right, step, 1, lstrip.at[lpart[k]], lft.at[k, lpart[k]], 3 + k))
        plan.append((left, step, -1, fstrip.at[fpart[k]], rgt.at[k, fpart[k]], 6 + k))
    above = {0: has_up, 1: has_down, 2: has_down}
    for k, there in enumerate((has_up, None, has_down)):
        above[3 + k] = has_left if there is None else has_left & there
        above[6 + k] = has_right if there is None else has_right & there
    zero_of = {0: top, 1: bot, 2: cbot}
    for k in range(3):
        zero_of[3 + k] = lft.at[k]
        zero_of[6 + k] = rgt.at[k]
    for n, ref in zero_of.items():

        @pl.when(jnp.logical_not(above[n]))
        def _(ref=ref):
            ref[...] = jnp.zeros(ref.shape, ref.dtype)

    for load in loads:
        load.wait()
    wt[:, 256:400] = wg[...]
    full[z, y, :, lanes] = wt[:, lanes]
    for h in range(2):
        side = slice(128 * h, 128 * h + 128)
        for r in range(16):
            image[h, (r + 1) * PW + 1 : (r + 1) * PW + 33] = regv[r, :, side].astype(F32)
        lstrip[:, side] = image[h, pl.ds(PW + 32, 16, stride=PW), :].astype(BF)
        for q in range(2):
            for e in range(2):
                fstrip[1 - e, :, 256 * q + 128 * h : 256 * q + 128 * h + 128] = image[
                    h, pl.ds((8 * e + 1) * PW + 1 + q, 8, stride=PW), :
                ].astype(BF)
    for h in range(4):
        side = slice(128 * h, 128 * h + 128)
        for i in range(8):
            c32[h, i * S : i * S + 16] = cotv[i, :, side].astype(F32)
        fstrip[2, :, side] = c32[h, pl.ds(0, 8, stride=S), :].astype(BF)

    pl.semaphore_wait(barrier, count)

    order = [nz // 2] + [n for d in range(nz // 2 - 1, 0, -1) for n in (d, nz - d)]
    late = order[:3]
    relayed = [d for d in [0] + order[::-1] if d not in late]
    along_z, upward, downward, forward = {}, {}, {}, {}
    for d in order:
        copy = remote(
            wt.at[:, lanes], full.at[z, y, :, lanes], zs.at[d], zr.at[d],
            row, lax.rem(z + d, nz) * NY + y,
        )
        copy.start()
        along_z[d] = copy

    def to_neighbours(d):
        here = full.at[lax.rem(z + nz - d, nz), y, :, lanes]
        upward[d] = remote(here, here, us.at[d], ur.at[d], row, z * NY + y_up)
        downward[d] = remote(here, here, ds.at[d], dr_.at[d], row, z * NY + y_down)
        if d in late:
            forward[d] = remote(here, here, fs.at[d], fr.at[d], row, z * NY + y_far)
            forward[d].start()
        upward[d].start()
        downward[d].start()

    to_neighbours(0)
    halos = []
    for there, dr, dc, src, dst, n in plan:
        copy = remote(src, dst, hs.at[n], hr.at[n], row + dr, col + dc)
        halos.append((there, copy, n))

        @pl.when(there)
        def _(copy=copy):
            copy.start()

    nearest = [0] + order[::-1]
    for d in nearest[1:]:
        along_z[d].wait_recv()
        to_neighbours(d)

    columns = []

    def column(at):
        block = full.at[:, at, :, lanes]
        n = len(columns)
        copy = remote(block, block, cs.at[n], cr.at[n], partner, col)
        copy.start()
        columns.append(copy)

    column(y)

    for d in nearest:
        b = lax.rem(z + nz - d, nz)
        upward[d].wait_recv()
        if d in relayed[::2]:
            here = full.at[b, y_down, :, lanes]
            forward[d] = remote(here, here, fs.at[d], fr.at[d], row, z * NY + y_up)
            forward[d].start()
        downward[d].wait_recv()
        if d in relayed[1::2]:
            here = full.at[b, y_up, :, lanes]
            forward[d] = remote(here, here, fs.at[d], fr.at[d], row, z * NY + y_down)
            forward[d].start()
    column(y_up)
    column(y_down)

    for there, copy, n in halos:

        @pl.when(above[n])
        def _(copy=copy):
            copy.wait_recv()

    for h in range(2):
        side = slice(128 * h, 128 * h + 128)
        image[h, 1:33] = top[:, side].astype(F32)
        for r in range(2):
            image[h, (17 + r) * PW + 1 : (17 + r) * PW + 33] = bot[r, :, side].astype(F32)
        image[h, pl.ds(PW, 16, stride=PW), :] = lft[1, :, side].astype(F32)
        image[h, 0:1] = lft[0, 8:16, side].astype(F32)[7:8]
        below = lft[2, 0:8, side].astype(F32)
        for r in range(2):
            image[h, (17 + r) * PW : (17 + r) * PW + 1] = below[r : r + 1]
        for q in range(2):
            side = slice(256 * q + 128 * h, 256 * q + 128 * h + 128)
            for e in range(2):
                low = (8 * e + 1) * PW + 33 + q
                image[h, pl.ds(low, 8, stride=PW), :] = rgt[1, 1 - e, :, side].astype(F32)
            image[h, 33 + q : 34 + q] = rgt[0, 0, :, side].astype(F32)[7:8]
            corner = rgt[2, 1, :, side].astype(F32)
            for r in range(2):
                low = (17 + r) * PW + 33 + q
                image[h, low : low + 1] = corner[r : r + 1]
    for h in range(4):
        side = slice(128 * h, 128 * h + 128)
        c32[h, 8 * S : 8 * S + 16] = cbot[:, side].astype(F32)
        c32[h, pl.ds(16, 8, stride=S), :] = rgt[1, 2, :, side].astype(F32)
        c32[h, 8 * S + 16 : 8 * S + 17] = rgt[2, 2, :, side].astype(F32)[0:1]
    for k in range(4):
        pr, pc = divmod(k, 2)
        for i in range(10):
            for h in range(2):
                xp[k, i * S : (i + 1) * S, 128 * h : 128 * h + 128] = image[
                    h, pl.ds((2 * i + pr) * PW + pc, S, stride=2), :
                ]

    for d in nearest:
        forward[d].wait_recv()
    column(y_far)
    for copy in columns:
        copy.wait_recv()

    front(full, xp, hid, sl1, bdt, h2, sl2)
    w_r = full[:, :, :, 0:256].reshape(512, 256)
    w_s = full[:, :, :, 512:768].reshape(512, 256)
    w_e = full[:, :, :, 768:1280].reshape(512, 512)
    mine = [pl.ds(pl.multiple_of(first + core * wide, 128), wide) for first, wide in CHUNKS]
    other = [pl.ds(pl.multiple_of(first + (1 - core) * wide, 128), wide) for first, wide in CHUNKS]
    chunks = (1, 0)

    across, along_y, turn_z, along_x = {}, {}, {}, {}

    def start_across(q):
        for n, at in enumerate((y_far, y_up, y_down, y)):
            copy = remote(
                gt.at[:, at, :, other[q]], rc.at[:, at, :, LOCAL[q]],
                rcs.at[q, n], rcr.at[q, n], partner, col,
            )
            copy.start()
            across[q, n] = copy

    def chip(q, n, at):
        return gt[n, at, :, mine[q]].astype(F32) + rc[n, at, :, LOCAL[q]].astype(F32)

    def start_y(q, n, to):
        copy = remote(
            send.at[n, :, :, LOCAL[q]], land.at[n, :, :, LOCAL[q]],
            rys.at[q, n], ryr.at[q, n], row, z * NY + to,
        )
        copy.start()
        along_y[q, n] = copy

    def fill(q, n, low, at, extra=None):
        for k in range(nh):
            term = chip(q, low + k, at)
            if extra is not None:
                term = term + land[extra, k, :, LOCAL[q]].astype(F32)
            send[n, k, :, LOCAL[q]] = term.astype(BF)

    def y_first(q):
        across[q, 0].wait_recv()
        fill(q, 0, 0, y_far)
        start_y(q, 0, y_up)
        fill(q, 1, nh, y_far)
        start_y(q, 1, y_down)
        across[q, 1].wait_recv()
        fill(q, 2, nh, y_up)
        start_y(q, 2, y_up)
        across[q, 2].wait_recv()
        fill(q, 3, 0, y_down)
        start_y(q, 3, y_down)

    def y_second(q):
        along_y[q, 0].wait_recv()
        fill(q, 4, 0, y_up, 0)
        start_y(q, 4, y_up)
        along_y[q, 1].wait_recv()
        fill(q, 5, nh, y_down, 1)
        start_y(q, 5, y_down)

    def put(first, lanes, value):
        blocks = value.reshape(value.shape[0] // (NY * GW), NY, GW, value.shape[1])
        gt[pl.ds(first // (NY * GW), blocks.shape[0]), :, :, lanes] = blocks.astype(BF)

    own = lax.rem(lax.broadcasted_iota(jnp.int32, (MW, 256), 0), S) < 16
    strided = xp[3, :MO].astype(BF)
    for n in range(2):
        half = slice(256 * n, 256 * n + 256)
        total = mm(h2[...], w_e[half], NT) + mm(strided, w_s[half], NT)
        gate = sigmoid(total)
        act = total * gate
        for i in range(8):
            block_out[i, :, half] = act[i * S : i * S + 16].astype(BF)
        cots = jnp.concatenate([c32[2 * n], c32[2 * n + 1]], axis=1)
        grad = cots * (gate + act * (1.0 - gate))
        gs[:, half] = grad.astype(BF)
        kept = jnp.where(own, grad[:MW], 0.0)
        gso[:, half] = kept.astype(BF)
        gsot[half, :] = jnp.transpose(kept).astype(BF)

    for n in range(2):
        half = slice(256 * n, 256 * n + 256)
        put(256 * n, slice(512, 768), mm(gsot[half, :], strided[:MW], NN))
        for m in range(2):
            cols = slice(256 * m, 256 * m + 256)
            put(256 * n, slice(768 + 256 * m, 1024 + 256 * m), mm(gsot[half, :], h2[:MW, cols], NN))
    start_across(1)

    for t in range(2):
        half = slice(256 * t, 256 * t + 256)
        grad = mm(gs[...], w_e[:, 256 * t : 256 * t + 256], NN) * sl2[:, half]
        g2[:, half] = grad.astype(BF).astype(F32)
        g2ot[half, :] = jnp.transpose(jnp.where(own, grad[:MW], 0.0)).astype(BF)

    lane = lax.broadcasted_iota(jnp.int32, (16, 128), 1) // GW
    for u in range(4):
        block = slice(128 * u, 128 * u + 128)
        sums = [[jnp.zeros((16, 128), F32)] * 8, [jnp.zeros((16, 128), F32)] * 8]
        for tap in range(9):
            k, off = tap_source(tap)
            outer = mm(g2ot[block, :], hid[k, off : off + MW, block].astype(BF), NN)
            for g in range(8):
                piece = outer[g * 16 : g * 16 + 16]
                turn = ((tap % 8 - g) * 16) % 128
                if turn:
                    piece = pltpu.roll(piece, turn, 1)
                sums[tap // 8][g] = jnp.where(lane == tap % 8, piece, sums[tap // 8][g])
        for h in range(2):
            for g in range(8):
                at = divmod(8 * u + g, NY)
                gt[at[0], at[1], :, 256 + 128 * h : 384 + 128 * h] = sums[h][g].astype(BF)


    y_first(1)

    for k in range(4):
        pr, pc = divmod(k, 2)
        window = (1 - pr) * S + (1 - pc)
        for t in range(2):
            half = slice(256 * t, 256 * t + 256)
            spread = jnp.zeros((MW, 256), F32)
            for tap in range(9):
                a, b = divmod(tap, 3)
                if tap_source(tap)[0] != k:
                    continue
                off = (a == 0) * S + (b == 0)
                spread = spread + mm(g2[off : off + MW, half].astype(BF), bdt[tap, t], NN)
            grad = jnp.where(own, spread * sl1[k, window : window + MW, half], 0.0)
            g1[k, :, half] = grad.astype(BF)
            g1t[k, half, :] = jnp.transpose(grad).astype(BF)
    for n in range(2):
        half = slice(256 * n, 256 * n + 256)
        grad = jnp.zeros((256, 256), F32)
        for k in range(4):
            pr, pc = divmod(k, 2)
            window = (1 - pr) * S + (1 - pc)
            grad = grad + mm(g1t[k, half, :], xp[k, window : window + MW].astype(BF), NN)
        put(256 * n, slice(0, 256), grad)
    start_across(0)

    for k in range(4):
        pr, pc = divmod(k, 2)
        back = mm(g1[k], w_r, NN)
        if k == 3:
            back = back + mm(gso[...], w_s, NN)
        for i in range(8):
            line = (2 * i + 1 - pr) * 32 + 1 - pc
            for h in range(2):
                rg[h, pl.ds(line, 16, stride=2), :] = back[
                    i * S : i * S + 16, 128 * h : 128 * h + 128
                ]
    y_first(0)
    y_second(1)
    for r in range(16):
        for h in range(2):
            region_grad[r, :, 128 * h : 128 * h + 128] = rg[h, 32 * r : 32 * r + 32].astype(BF)
    y_second(0)

    for q in chunks:
        part = LOCAL[q]
        across[q, 3].wait_recv()
        for n in (2, 3, 4, 5):
            along_y[q, n].wait_recv()
        for k in range(nh):
            s2[k, :, part] = (
                chip(q, k, y) + land[3, k, :, part].astype(F32) + land[4, k, :, part].astype(F32)
            )
            s2[nh + k, :, part] = (
                chip(q, nh + k, y) + land[2, k, :, part].astype(F32) + land[5, k, :, part].astype(F32)
            )
        for d in order:
            to = lax.rem(z + d, nz)
            rz[0, d, :, part] = s2[to, :, part].astype(BF)
            copy = remote(
                rz.at[0, d, :, part], rz.at[1, d, :, part], rzs.at[q, d], rzr.at[q, d], row, to * NY + y
            )
            copy.start()
            turn_z[q, d] = copy
    for q in chunks:
        part = LOCAL[q]
        term = s2[z, :, part]
        for d in range(1, nz):
            turn_z[q, d].wait_recv()
            term = term + rz[1, d, :, part].astype(F32)
        rx[x, :, mine[q]] = term.astype(BF)
        for d in range(1, nx):
            for e in range(2):
                here = rx.at[x, :, mine[q]]
                to = lax.rem(core + e, 2)
                copy = remote(
                    here, here, rxs.at[q, 2 * d + e], rxr.at[q, 2 * d + e],
                    2 * lax.rem(x + d, nx) + to, col,
                )
                copy.start()
                along_x[q, 2 * d + e] = copy
        here = rx.at[x, :, mine[q]]
        copy = remote(here, here, rxs.at[q, 1], rxr.at[q, 1], partner, col)
        copy.start()
        along_x[q, 1] = copy
    for copy in along_x.values():
        copy.wait_recv()
    term = rx[0].astype(F32)
    for n in range(1, nx):
        term = term + rx[n].astype(F32)
    out[...] = term
    for there, copy, n in halos:

        @pl.when(there)
        def _(copy=copy):
            copy.wait_send()

    for copy in columns:
        copy.wait_send()
    for group in (along_z, upward, downward, forward, across, along_y, turn_z, along_x):
        for copy in group.values():
            copy.wait_send()


def whole(nr, nc, *arrays):
    nz, nx = nc // NY, nr // 2
    kw = GW
    shape = jax.ShapeDtypeStruct
    hbm = pl.BlockSpec(memory_space=pltpu.HBM)
    dma = pltpu.SemaphoreType.DMA
    return pl.pallas_call(
        functools.partial(whole_kernel, nr, nc),
        out_shape=(
            shape((8, 16, 512), BF),
            shape((16, 32, 256), BF),
            shape((kw, LANES), F32),
        ),
        in_specs=[hbm] * 6,
        out_specs=(VMEM,) * 3,
        scratch_shapes=[
            pltpu.VMEM((nz, NY, kw, LANES), BF),
            pltpu.VMEM((4, 10 * S, 256), F32),
            pltpu.VMEM((4, MO, 128), F32),
            pltpu.VMEM((4, PLANE, 512), F32),
            pltpu.VMEM((4, PLANE, 512), F32),
            pltpu.VMEM((9, 2, 256, 256), BF),
            pltpu.VMEM((MO, 512), BF),
            pltpu.VMEM((MO, 512), F32),
            pltpu.VMEM((kw, LANES), BF),
            pltpu.VMEM((kw, 144), BF),
            pltpu.VMEM((16, 32, 256), BF),
            pltpu.VMEM((8, 16, 512), BF),
            pltpu.VMEM((2, 20 * PW, 128), F32),
            pltpu.VMEM((16, 256), BF),
            pltpu.VMEM((3, 8, 512), BF),
            pltpu.VMEM((32, 256), BF),
            pltpu.VMEM((2, 32, 256), BF),
            pltpu.VMEM((16, 512), BF),
            pltpu.VMEM((3, 16, 256), BF),
            pltpu.VMEM((3, 3, 8, 512), BF),
            pltpu.VMEM((512, MW), BF),
            pltpu.VMEM((512, MW), BF),
            pltpu.VMEM((4, 512, MW), BF),
            pltpu.VMEM((MO, 512), BF),
            pltpu.VMEM((MW, 512), BF),
            pltpu.VMEM((MO, 512), F32),
            pltpu.VMEM((4, MW, 512), BF),
            pltpu.VMEM((2, 512, 128), F32),
            pltpu.VMEM((nz, NY, kw, LANES), BF),
            pltpu.VMEM((nz, NY, kw, HALF), BF),
            pltpu.VMEM((6, nz // 2, kw, HALF), BF),
            pltpu.VMEM((6, nz // 2, kw, HALF), BF),
            pltpu.VMEM((nz, kw, HALF), F32),
            pltpu.VMEM((2, nz, kw, HALF), BF),
            pltpu.VMEM((nx, kw, LANES), BF),
            dma((6,)),
            dma((nz,)), dma((nz,)), dma((nz,)), dma((nz,)),
            dma((nz,)), dma((nz,)), dma((nz,)), dma((nz,)),
            dma((4,)), dma((4,)), dma((9,)), dma((9,)),
            dma((2, 4)), dma((2, 4)), dma((2, 6)), dma((2, 6)),
            dma((2, nz)), dma((2, nz)), dma((2, nr)), dma((2, nr)),
        ],
        compiler_params=pltpu.CompilerParams(
            collective_id=0, has_side_effects=True, vmem_limit_bytes=48 << 20
        ),
        name="whole",
    )(*(pltpu.with_memory_space_constraint(a, pltpu.HBM) for a in arrays))


def store_kernel(
    block_out, region_grad, slab,
    block_to, region_to, reduce_grad, group_grad, expand_grad, shortcut_grad, group, sems,
):
    pairs = [
        (region_grad, region_to),
        (block_out, block_to),
        (slab.at[:, 768:1280], expand_grad),
        (slab.at[:, 0:256], reduce_grad),
        (slab.at[:, 512:768], shortcut_grad),
        (group, group_grad),
    ]
    copies = [pltpu.make_async_copy(a, b, sems.at[n]) for n, (a, b) in enumerate(pairs)]
    for copy in copies[:-1]:
        copy.start()
    group[...] = slab[:, 256:400]
    copies[-1].start()
    for copy in copies:
        copy.wait()


def store(block_out, region_grad, slab):
    kw = slab.shape[0]
    shape = jax.ShapeDtypeStruct
    return pl.pallas_call(
        store_kernel,
        out_shape=(
            shape(block_out.shape, BF),
            shape(region_grad.shape, BF),
            *(shape((kw, n), F32) for n in (256, 144, 512, 256)),
        ),
        in_specs=[VMEM] * 3,
        out_specs=(pl.BlockSpec(memory_space=pltpu.HBM),) * 6,
        scratch_shapes=[pltpu.VMEM((kw, 144), F32), pltpu.SemaphoreType.DMA((6,))],
        compiler_params=pltpu.CompilerParams(vmem_limit_bytes=4 << 20),
        name="store",
    )(block_out, region_grad, slab)


def solution(mesh):
    nr, nc = mesh.shape["row"], mesh.shape["col"]

    def per_device(region, reduce_weight, group_weight, expand_weight, shortcut_weight, cotangent):
        block_out, region_grad, *grads = store(
            *whole(
                nr, nc, reduce_weight.T, group_weight.T, expand_weight.T, shortcut_weight.T,
                region, cotangent,
            )
        )
        return (block_out, region_grad, *(grad.T for grad in grads))

    weight = P(None, "col")
    tile = P("row", "col", None)
    return jax.shard_map(
        per_device,
        mesh=mesh,
        in_specs=(tile, weight, weight, weight, weight, tile),
        out_specs=(tile, tile, weight, weight, weight, weight),
        check_vma=False,
    )
```

```python
import functools

import jax
import jax.numpy as jnp
from jax import lax
from jax.experimental import pallas as pl
from jax.experimental.pallas import tpu as pltpu
from jax.sharding import PartitionSpec as P

MESH = pl.DeviceIdType.MESH
BF = jnp.bfloat16
F32 = jnp.float32
NY = 4
GW = 16
LANES = 1280
HALF = LANES // 2
CHUNKS = ((0, 256), (512, 384))
LOCAL = (slice(0, 256), slice(256, 640))
S = 24
PLANE = 256
MO = 224
MW = 192
PW = 48
VMEM = pl.BlockSpec(memory_space=pltpu.VMEM)

NN = (((1,), (0,)), ((), ()))
NT = (((1,), (1,)), ((), ()))
TN = (((0,), (0,)), ((), ()))


def mm(lhs, rhs, dims):
    return lax.dot_general(lhs, rhs, dims, preferred_element_type=F32)


def sigmoid(value):
    return 0.5 * jnp.tanh(0.5 * value) + 0.5


def remote(src, dst, send_sem, recv_sem, row, col):
    return pltpu.make_async_remote_copy(
        src_ref=src,
        dst_ref=dst,
        send_sem=send_sem,
        recv_sem=recv_sem,
        device_id=(row, col),
        device_id_type=MESH,
    )


def tap_source(tap):
    a, b = divmod(tap, 3)
    plane = (a % 2) * 2 + b % 2
    return plane, (a == 2) * S + (b == 2)


def front(full, xp, hid, sl1, bdt, h2, sl2):
    weight = full[:, :, :, 0:256].reshape(512, 256)
    for k in range(4):
        hid[k, 10 * S :] = jnp.zeros((PLANE - 10 * S, 512), F32)
        pixels = xp[k].astype(BF)
        for n in range(2):
            half = slice(256 * n, 256 * n + 256)
            pre = mm(pixels, weight[half], NT)
            gate = sigmoid(pre)
            act = pre * gate
            hid[k, : 10 * S, half] = act.astype(BF).astype(F32)
            sl1[k, : 10 * S, half] = gate + act * (1.0 - gate)

    lane = lax.broadcasted_iota(jnp.int32, (16, 128), 1) // GW
    for tap in range(9):
        first = 256 + 128 * (tap // 8)
        for u in range(4):
            t, v = divmod(u, 2)
            for g in range(8):
                at = divmod(8 * u + g, NY)
                piece = full[at[0], at[1], :, first : first + 128].astype(F32)
                turn = ((g - tap % 8) * 16) % 128
                if turn:
                    piece = pltpu.roll(piece, turn, 1)
                piece = jnp.where(lane == g, piece, 0.0).astype(BF)
                low = v * 128 + g * 16
                bdt[tap, t, low : low + 16, v * 128 : v * 128 + 128] = piece

    for t in range(2):
        half = slice(256 * t, 256 * t + 256)
        pre = jnp.zeros((MO, 256), F32)
        for tap in range(9):
            k, off = tap_source(tap)
            pre = pre + mm(hid[k, off : off + MO, half].astype(BF), bdt[tap, t], NT)
        gate = sigmoid(pre)
        act = pre * gate
        h2[:, half] = act.astype(BF)
        sl2[:, half] = gate + act * (1.0 - gate)


def whole_kernel(
    nr, nc, w_reduce, w_group, w_expand, w_short, region, cot,
    block_out, region_grad, out,
    full, xp, c32, hid, sl1, bdt, h2, sl2, wt, wg, regv, cotv, image, lstrip, fstrip, top, bot, cbot, lft, rgt,
    g2o, gs, gso, g2, g1, rg, gt, rc, send, land, s2, rz, rx,
    ls, zs, zr, us, ur, ds, dr_, fs, fr, cs, cr, hs, hr,
    rcs, rcr, rys, ryr, rzs, rzr, rxs, rxr,
):
    nz, nx, nh = nc // NY, nr // 2, nc // NY // 2
    row, col = lax.axis_index("row"), lax.axis_index("col")
    x, core = row // 2, lax.rem(row, 2)
    partner = row + 1 - 2 * core
    z, y = col // NY, lax.rem(col, NY)
    y_up, y_down, y_far = lax.rem(y + 1, NY), lax.rem(y + NY - 1, NY), lax.rem(y + 2, NY)
    lanes = pl.ds(pl.multiple_of(core * HALF, 128), HALF)
    has_up, has_down = row > 0, row < nr - 1
    has_left, has_right = col > 0, col < nc - 1

    barrier = pltpu.get_barrier_semaphore()

    def greet(to_row, to_col):
        pl.semaphore_signal(barrier, inc=1, device_id=(to_row, to_col), device_id_type=MESH)

    for d in range(1, nz):
        greet(row, lax.rem(z + d, nz) * NY + y)
    greet(row, z * NY + y_up)
    greet(row, z * NY + y_down)
    greet(row, z * NY + y_far)
    greet(partner, col)
    for d in range(1, nx):
        greet(2 * lax.rem(x + d, nx), col)
        greet(2 * lax.rem(x + d, nx) + 1, col)
    count = nz + 3 + 2 * (nx - 1)
    for dr in (-1, 0, 1):
        for dc in (-1, 0, 1):
            if dr == 0 and dc == 0:
                continue
            there = None
            for step, less, more in ((dr, has_up, has_down), (dc, has_left, has_right)):
                if step:
                    flag = more if step > 0 else less
                    there = flag if there is None else there & flag
            count = count + there.astype(jnp.int32)

            @pl.when(there)
            def _(dr=dr, dc=dc):
                greet(row + dr, col + dc)

    loads = [
        pltpu.make_async_copy(region, regv, ls.at[0]),
        pltpu.make_async_copy(cot, cotv, ls.at[1]),
        pltpu.make_async_copy(w_reduce, wt.at[:, 0:256], ls.at[2]),
        pltpu.make_async_copy(w_short, wt.at[:, 512:768], ls.at[3]),
        pltpu.make_async_copy(w_expand, wt.at[:, 768:1280], ls.at[4]),
        pltpu.make_async_copy(w_group, wg, ls.at[5]),
    ]
    for load in loads:
        load.start()
    wt[:, 256:512] = jnp.zeros((wt.shape[0], 256), BF)
    image[...] = jnp.zeros_like(image)
    bdt[...] = jnp.zeros_like(bdt)
    c32[...] = jnp.zeros_like(c32)

    lpart = (pl.ds(8, 8), pl.ds(0, 16), pl.ds(0, 8))
    fpart = (pl.ds(0, 1), pl.ds(0, 3), pl.ds(1, 2))
    plan = [
        (has_down, 1, 0, regv.at[15], top, 0),
        (has_up, -1, 0, regv.at[pl.ds(0, 2)], bot, 1),
        (has_up, -1, 0, cotv.at[0], cbot, 2),
    ]
    for k, (there, step) in enumerate(((has_down, 1), (None, 0), (has_up, -1))):
        right = has_right if there is None else has_right & there
        left = has_left if there is None else has_left & there
        plan.append((right, step, 1, lstrip.at[lpart[k]], lft.at[k, lpart[k]], 3 + k))
        plan.append((left, step, -1, fstrip.at[fpart[k]], rgt.at[k, fpart[k]], 6 + k))
    above = {0: has_up, 1: has_down, 2: has_down}
    for k, there in enumerate((has_up, None, has_down)):
        above[3 + k] = has_left if there is None else has_left & there
        above[6 + k] = has_right if there is None else has_right & there
    zero_of = {0: top, 1: bot, 2: cbot}
    for k in range(3):
        zero_of[3 + k] = lft.at[k]
        zero_of[6 + k] = rgt.at[k]
    for n, ref in zero_of.items():

        @pl.when(jnp.logical_not(above[n]))
        def _(ref=ref):
            ref[...] = jnp.zeros(ref.shape, ref.dtype)

    for load in loads:
        load.wait()
    wt[:, 256:400] = wg[...]
    full[z, y, :, lanes] = wt[:, lanes]
    for h in range(2):
        side = slice(128 * h, 128 * h + 128)
        for r in range(16):
            image[h, (r + 1) * PW + 1 : (r + 1) * PW + 33] = regv[r, :, side].astype(F32)
        lstrip[:, side] = image[h, pl.ds(PW + 32, 16, stride=PW), :].astype(BF)
        for q in range(2):
            for e in range(2):
                fstrip[1 - e, :, 256 * q + 128 * h : 256 * q + 128 * h + 128] = image[
                    h, pl.ds((8 * e + 1) * PW + 1 + q, 8, stride=PW), :
                ].astype(BF)
    for h in range(4):
        side = slice(128 * h, 128 * h + 128)
        for i in range(8):
            c32[h, i * S : i * S + 16] = cotv[i, :, side].astype(F32)
        fstrip[2, :, side] = c32[h, pl.ds(0, 8, stride=S), :].astype(BF)

    pl.semaphore_wait(barrier, count)

    order = [nz // 2] + [n for d in range(nz // 2 - 1, 0, -1) for n in (d, nz - d)]
    across_x = [nx // 2] + [n for d in range(nx // 2 - 1, 0, -1) for n in (d, nx - d)]
    late = order[:3]
    relayed = [d for d in [0] + order[::-1] if d not in late]
    along_z, upward, downward, forward = {}, {}, {}, {}
    for d in order[::-1]:
        copy = remote(
            wt.at[:, lanes], full.at[z, y, :, lanes], zs.at[d], zr.at[d],
            row, lax.rem(z + d, nz) * NY + y,
        )
        copy.start()
        along_z[d] = copy

    def to_neighbours(d):
        here = full.at[lax.rem(z + nz - d, nz), y, :, lanes]
        upward[d] = remote(here, here, us.at[d], ur.at[d], row, z * NY + y_up)
        downward[d] = remote(here, here, ds.at[d], dr_.at[d], row, z * NY + y_down)
        if d in late:
            forward[d] = remote(here, here, fs.at[d], fr.at[d], row, z * NY + y_far)
            forward[d].start()
        upward[d].start()
        downward[d].start()

    to_neighbours(0)
    halos = []
    for there, dr, dc, src, dst, n in plan:
        copy = remote(src, dst, hs.at[n], hr.at[n], row + dr, col + dc)
        halos.append((there, copy, n))

        @pl.when(there)
        def _(copy=copy):
            copy.start()

    nearest = [0] + order[::-1]
    for d in nearest[1:]:
        along_z[d].wait_recv()
        to_neighbours(d)

    columns = []

    def column(at):
        block = full.at[:, at, :, lanes]
        n = len(columns)
        copy = remote(block, block, cs.at[n], cr.at[n], partner, col)
        copy.start()
        columns.append(copy)

    column(y)

    for d in nearest:
        b = lax.rem(z + nz - d, nz)
        upward[d].wait_recv()
        if d in relayed[::2]:
            here = full.at[b, y_down, :, lanes]
            forward[d] = remote(here, here, fs.at[d], fr.at[d], row, z * NY + y_up)
            forward[d].start()
        downward[d].wait_recv()
        if d in relayed[1::2]:
            here = full.at[b, y_up, :, lanes]
            forward[d] = remote(here, here, fs.at[d], fr.at[d], row, z * NY + y_down)
            forward[d].start()
    column(y_up)
    column(y_down)

    for there, copy, n in halos:

        @pl.when(above[n])
        def _(copy=copy):
            copy.wait_recv()

    for h in range(2):
        side = slice(128 * h, 128 * h + 128)
        image[h, 1:33] = top[:, side].astype(F32)
        for r in range(2):
            image[h, (17 + r) * PW + 1 : (17 + r) * PW + 33] = bot[r, :, side].astype(F32)
        image[h, pl.ds(PW, 16, stride=PW), :] = lft[1, :, side].astype(F32)
        image[h, 0:1] = lft[0, 8:16, side].astype(F32)[7:8]
        below = lft[2, 0:8, side].astype(F32)
        for r in range(2):
            image[h, (17 + r) * PW : (17 + r) * PW + 1] = below[r : r + 1]
        for q in range(2):
            side = slice(256 * q + 128 * h, 256 * q + 128 * h + 128)
            for e in range(2):
                low = (8 * e + 1) * PW + 33 + q
                image[h, pl.ds(low, 8, stride=PW), :] = rgt[1, 1 - e, :, side].astype(F32)
            image[h, 33 + q : 34 + q] = rgt[0, 0, :, side].astype(F32)[7:8]
            corner = rgt[2, 1, :, side].astype(F32)
            for r in range(2):
                low = (17 + r) * PW + 33 + q
                image[h, low : low + 1] = corner[r : r + 1]
    for h in range(4):
        side = slice(128 * h, 128 * h + 128)
        c32[h, 8 * S : 8 * S + 16] = cbot[:, side].astype(F32)
        c32[h, pl.ds(16, 8, stride=S), :] = rgt[1, 2, :, side].astype(F32)
        c32[h, 8 * S + 16 : 8 * S + 17] = rgt[2, 2, :, side].astype(F32)[0:1]
    for k in range(4):
        pr, pc = divmod(k, 2)
        for i in range(10):
            for h in range(2):
                xp[k, i * S : (i + 1) * S, 128 * h : 128 * h + 128] = image[
                    h, pl.ds((2 * i + pr) * PW + pc, S, stride=2), :
                ]

    for d in nearest:
        forward[d].wait_recv()
    column(y_far)
    for copy in columns:
        copy.wait_recv()

    front(full, xp, hid, sl1, bdt, h2, sl2)
    w_r = full[:, :, :, 0:256].reshape(512, 256)
    w_s = full[:, :, :, 512:768].reshape(512, 256)
    w_e = full[:, :, :, 768:1280].reshape(512, 512)
    mine = [pl.ds(pl.multiple_of(first + core * wide, 128), wide) for first, wide in CHUNKS]
    other = [pl.ds(pl.multiple_of(first + (1 - core) * wide, 128), wide) for first, wide in CHUNKS]
    chunks = (1, 0)

    across, along_y, turn_z, along_x = {}, {}, {}, {}

    def start_across(q):
        for n, at in enumerate((y_far, y_up, y_down, y)):
            copy = remote(
                gt.at[:, at, :, other[q]], rc.at[:, at, :, LOCAL[q]],
                rcs.at[q, n], rcr.at[q, n], partner, col,
            )
            copy.start()
            across[q, n] = copy

    def chip(q, n, at):
        return gt[n, at, :, mine[q]].astype(F32) + rc[n, at, :, LOCAL[q]].astype(F32)

    def start_y(q, n, to):
        copy = remote(
            send.at[n, :, :, LOCAL[q]], land.at[n, :, :, LOCAL[q]],
            rys.at[q, n], ryr.at[q, n], row, z * NY + to,
        )
        copy.start()
        along_y[q, n] = copy

    def fill(q, n, low, at, extra=None):
        for k in range(nh):
            term = chip(q, low + k, at)
            if extra is not None:
                term = term + land[extra, k, :, LOCAL[q]].astype(F32)
            send[n, k, :, LOCAL[q]] = term.astype(BF)

    def y_first(q):
        across[q, 0].wait_recv()
        fill(q, 0, 0, y_far)
        start_y(q, 0, y_up)
        fill(q, 1, nh, y_far)
        start_y(q, 1, y_down)
        across[q, 1].wait_recv()
        fill(q, 2, nh, y_up)
        start_y(q, 2, y_up)
        across[q, 2].wait_recv()
        fill(q, 3, 0, y_down)
        start_y(q, 3, y_down)

    def y_second(q):
        along_y[q, 0].wait_recv()
        fill(q, 4, 0, y_up, 0)
        start_y(q, 4, y_up)
        along_y[q, 1].wait_recv()
        fill(q, 5, nh, y_down, 1)
        start_y(q, 5, y_down)

    def put(first, lanes, value):
        blocks = value.reshape(value.shape[0] // (NY * GW), NY, GW, value.shape[1])
        gt[pl.ds(first // (NY * GW), blocks.shape[0]), :, :, lanes] = blocks.astype(BF)

    own = lax.rem(lax.broadcasted_iota(jnp.int32, (MW, 256), 0), S) < 16
    strided = xp[3, :MO].astype(BF)
    for n in range(2):
        half = slice(256 * n, 256 * n + 256)
        total = mm(h2[...], w_e[half], NT) + mm(strided, w_s[half], NT)
        gate = sigmoid(total)
        act = total * gate
        for i in range(8):
            block_out[i, :, half] = act[i * S : i * S + 16].astype(BF)
        cots = jnp.concatenate([c32[2 * n], c32[2 * n + 1]], axis=1)
        grad = cots * (gate + act * (1.0 - gate))
        gs[:, half] = grad.astype(BF)
        gso[:, half] = jnp.where(own, grad[:MW], 0.0).astype(BF)

    for n in range(2):
        half = slice(256 * n, 256 * n + 256)
        put(256 * n, slice(512, 768), mm(gso[:, half], strided[:MW], TN))
        for m in range(2):
            cols = slice(256 * m, 256 * m + 256)
            put(256 * n, slice(768 + 256 * m, 1024 + 256 * m), mm(gso[:, half], h2[:MW, cols], TN))
    start_across(1)

    for t in range(2):
        half = slice(256 * t, 256 * t + 256)
        grad = mm(gs[...], w_e[:, 256 * t : 256 * t + 256], NN) * sl2[:, half]
        g2[:, half] = grad.astype(BF).astype(F32)
        g2o[:, half] = jnp.where(own, grad[:MW], 0.0).astype(BF)

    lane = lax.broadcasted_iota(jnp.int32, (16, 128), 1) // GW
    for u in range(4):
        block = slice(128 * u, 128 * u + 128)
        sums = [[jnp.zeros((16, 128), F32)] * 8, [jnp.zeros((16, 128), F32)] * 8]
        for tap in range(9):
            k, off = tap_source(tap)
            outer = mm(g2o[:, block], hid[k, off : off + MW, block].astype(BF), TN)
            for g in range(8):
                piece = outer[g * 16 : g * 16 + 16]
                turn = ((tap % 8 - g) * 16) % 128
                if turn:
                    piece = pltpu.roll(piece, turn, 1)
                sums[tap // 8][g] = jnp.where(lane == tap % 8, piece, sums[tap // 8][g])
        for h in range(2):
            for g in range(8):
                at = divmod(8 * u + g, NY)
                gt[at[0], at[1], :, 256 + 128 * h : 384 + 128 * h] = sums[h][g].astype(BF)


    y_first(1)

    for k in range(4):
        pr, pc = divmod(k, 2)
        window = (1 - pr) * S + (1 - pc)
        for t in range(2):
            half = slice(256 * t, 256 * t + 256)
            spread = jnp.zeros((MW, 256), F32)
            for tap in range(9):
                a, b = divmod(tap, 3)
                if tap_source(tap)[0] != k:
                    continue
                off = (a == 0) * S + (b == 0)
                spread = spread + mm(g2[off : off + MW, half].astype(BF), bdt[tap, t], NN)
            grad = jnp.where(own, spread * sl1[k, window : window + MW, half], 0.0)
            g1[k, :, half] = grad.astype(BF)
    for n in range(2):
        half = slice(256 * n, 256 * n + 256)
        grad = jnp.zeros((256, 256), F32)
        for k in range(4):
            pr, pc = divmod(k, 2)
            window = (1 - pr) * S + (1 - pc)
            grad = grad + mm(g1[k, :, half], xp[k, window : window + MW].astype(BF), TN)
        put(256 * n, slice(0, 256), grad)
    start_across(0)

    for k in range(4):
        pr, pc = divmod(k, 2)
        back = mm(g1[k], w_r, NN)
        if k == 3:
            back = back + mm(gso[...], w_s, NN)
        for i in range(8):
            line = (2 * i + 1 - pr) * 32 + 1 - pc
            for h in range(2):
                rg[h, pl.ds(line, 16, stride=2), :] = back[
                    i * S : i * S + 16, 128 * h : 128 * h + 128
                ]
    y_first(0)
    y_second(1)
    for r in range(16):
        for h in range(2):
            region_grad[r, :, 128 * h : 128 * h + 128] = rg[h, 32 * r : 32 * r + 32].astype(BF)
    y_second(0)

    for q in chunks:
        part = LOCAL[q]
        across[q, 3].wait_recv()
        for n in (2, 3, 4, 5):
            along_y[q, n].wait_recv()
        for k in range(nh):
            s2[k, :, part] = (
                chip(q, k, y) + land[3, k, :, part].astype(F32) + land[4, k, :, part].astype(F32)
            )
            s2[nh + k, :, part] = (
                chip(q, nh + k, y) + land[2, k, :, part].astype(F32) + land[5, k, :, part].astype(F32)
            )
        for d in order:
            to = lax.rem(z + d, nz)
            rz[0, d, :, part] = s2[to, :, part].astype(BF)
            copy = remote(
                rz.at[0, d, :, part], rz.at[1, d, :, part], rzs.at[q, d], rzr.at[q, d], row, to * NY + y
            )
            copy.start()
            turn_z[q, d] = copy
    for q in chunks:
        part = LOCAL[q]
        term = s2[z, :, part]
        for d in range(1, nz):
            turn_z[q, d].wait_recv()
            term = term + rz[1, d, :, part].astype(F32)
        rx[x, :, mine[q]] = term.astype(BF)
        for d in across_x:
            for e in range(2):
                here = rx.at[x, :, mine[q]]
                to = lax.rem(core + e, 2)
                copy = remote(
                    here, here, rxs.at[q, 2 * d + e], rxr.at[q, 2 * d + e],
                    2 * lax.rem(x + d, nx) + to, col,
                )
                copy.start()
                along_x[q, 2 * d + e] = copy
        here = rx.at[x, :, mine[q]]
        copy = remote(here, here, rxs.at[q, 1], rxr.at[q, 1], partner, col)
        copy.start()
        along_x[q, 1] = copy
    for copy in along_x.values():
        copy.wait_recv()
    term = rx[0].astype(F32)
    for n in range(1, nx):
        term = term + rx[n].astype(F32)
    out[...] = term
    for there, copy, n in halos:

        @pl.when(there)
        def _(copy=copy):
            copy.wait_send()

    for copy in columns:
        copy.wait_send()
    for group in (along_z, upward, downward, forward, across, along_y, turn_z, along_x):
        for copy in group.values():
            copy.wait_send()


def whole(nr, nc, *arrays):
    nz, nx = nc // NY, nr // 2
    kw = GW
    shape = jax.ShapeDtypeStruct
    hbm = pl.BlockSpec(memory_space=pltpu.HBM)
    dma = pltpu.SemaphoreType.DMA
    return pl.pallas_call(
        functools.partial(whole_kernel, nr, nc),
        out_shape=(
            shape((8, 16, 512), BF),
            shape((16, 32, 256), BF),
            shape((kw, LANES), F32),
        ),
        in_specs=[hbm] * 6,
        out_specs=(VMEM,) * 3,
        scratch_shapes=[
            pltpu.VMEM((nz, NY, kw, LANES), BF),
            pltpu.VMEM((4, 10 * S, 256), F32),
            pltpu.VMEM((4, MO, 128), F32),
            pltpu.VMEM((4, PLANE, 512), F32),
            pltpu.VMEM((4, PLANE, 512), F32),
            pltpu.VMEM((9, 2, 256, 256), BF),
            pltpu.VMEM((MO, 512), BF),
            pltpu.VMEM((MO, 512), F32),
            pltpu.VMEM((kw, LANES), BF),
            pltpu.VMEM((kw, 144), BF),
            pltpu.VMEM((16, 32, 256), BF),
            pltpu.VMEM((8, 16, 512), BF),
            pltpu.VMEM((2, 20 * PW, 128), F32),
            pltpu.VMEM((16, 256), BF),
            pltpu.VMEM((3, 8, 512), BF),
            pltpu.VMEM((32, 256), BF),
            pltpu.VMEM((2, 32, 256), BF),
            pltpu.VMEM((16, 512), BF),
            pltpu.VMEM((3, 16, 256), BF),
            pltpu.VMEM((3, 3, 8, 512), BF),
            pltpu.VMEM((MW, 512), BF),
            pltpu.VMEM((MO, 512), BF),
            pltpu.VMEM((MW, 512), BF),
            pltpu.VMEM((MO, 512), F32),
            pltpu.VMEM((4, MW, 512), BF),
            pltpu.VMEM((2, 512, 128), F32),
            pltpu.VMEM((nz, NY, kw, LANES), BF),
            pltpu.VMEM((nz, NY, kw, HALF), BF),
            pltpu.VMEM((6, nz // 2, kw, HALF), BF),
            pltpu.VMEM((6, nz // 2, kw, HALF), BF),
            pltpu.VMEM((nz, kw, HALF), F32),
            pltpu.VMEM((2, nz, kw, HALF), BF),
            pltpu.VMEM((nx, kw, LANES), BF),
            dma((6,)),
            dma((nz,)), dma((nz,)), dma((nz,)), dma((nz,)),
            dma((nz,)), dma((nz,)), dma((nz,)), dma((nz,)),
            dma((4,)), dma((4,)), dma((9,)), dma((9,)),
            dma((2, 4)), dma((2, 4)), dma((2, 6)), dma((2, 6)),
            dma((2, nz)), dma((2, nz)), dma((2, nr)), dma((2, nr)),
        ],
        compiler_params=pltpu.CompilerParams(
            collective_id=0, has_side_effects=True, vmem_limit_bytes=48 << 20
        ),
        name="whole",
    )(*(pltpu.with_memory_space_constraint(a, pltpu.HBM) for a in arrays))


def store_kernel(
    block_out, region_grad, slab,
    block_to, region_to, reduce_grad, group_grad, expand_grad, shortcut_grad, group, sems,
):
    pairs = [
        (region_grad, region_to),
        (block_out, block_to),
        (slab.at[:, 768:1280], expand_grad),
        (slab.at[:, 0:256], reduce_grad),
        (slab.at[:, 512:768], shortcut_grad),
        (group, group_grad),
    ]
    copies = [pltpu.make_async_copy(a, b, sems.at[n]) for n, (a, b) in enumerate(pairs)]
    for copy in copies[:-1]:
        copy.start()
    group[...] = slab[:, 256:400]
    copies[-1].start()
    for copy in copies:
        copy.wait()


def store(block_out, region_grad, slab):
    kw = slab.shape[0]
    shape = jax.ShapeDtypeStruct
    return pl.pallas_call(
        store_kernel,
        out_shape=(
            shape(block_out.shape, BF),
            shape(region_grad.shape, BF),
            *(shape((kw, n), F32) for n in (256, 144, 512, 256)),
        ),
        in_specs=[VMEM] * 3,
        out_specs=(pl.BlockSpec(memory_space=pltpu.HBM),) * 6,
        scratch_shapes=[pltpu.VMEM((kw, 144), F32), pltpu.SemaphoreType.DMA((6,))],
        compiler_params=pltpu.CompilerParams(vmem_limit_bytes=4 << 20),
        name="store",
    )(block_out, region_grad, slab)


def solution(mesh):
    nr, nc = mesh.shape["row"], mesh.shape["col"]

    def per_device(region, reduce_weight, group_weight, expand_weight, shortcut_weight, cotangent):
        block_out, region_grad, *grads = store(
            *whole(
                nr, nc, reduce_weight.T, group_weight.T, expand_weight.T, shortcut_weight.T,
                region, cotangent,
            )
        )
        return (block_out, region_grad, *(grad.T for grad in grads))

    weight = P(None, "col")
    tile = P("row", "col", None)
    return jax.shard_map(
        per_device,
        mesh=mesh,
        in_specs=(tile, weight, weight, weight, weight, tile),
        out_specs=(tile, tile, weight, weight, weight, weight),
        check_vma=False,
    )
```

```python
import functools

import jax
import jax.numpy as jnp
from jax import lax
from jax.experimental import pallas as pl
from jax.experimental.pallas import tpu as pltpu
from jax.sharding import PartitionSpec as P

MESH = pl.DeviceIdType.MESH
BF = jnp.bfloat16
F32 = jnp.float32
NY = 4
GW = 16
LANES = 1280
HALF = LANES // 2
CHUNKS = ((0, 256), (512, 384))
LOCAL = (slice(0, 256), slice(256, 640))
S = 24
PLANE = 256
MO = 224
MW = 192
PW = 48
VMEM = pl.BlockSpec(memory_space=pltpu.VMEM)

NN = (((1,), (0,)), ((), ()))
NT = (((1,), (1,)), ((), ()))
TN = (((0,), (0,)), ((), ()))


def mm(lhs, rhs, dims):
    return lax.dot_general(lhs, rhs, dims, preferred_element_type=F32)


def sigmoid(value):
    return 0.5 * jnp.tanh(0.5 * value) + 0.5


def remote(src, dst, send_sem, recv_sem, row, col):
    return pltpu.make_async_remote_copy(
        src_ref=src,
        dst_ref=dst,
        send_sem=send_sem,
        recv_sem=recv_sem,
        device_id=(row, col),
        device_id_type=MESH,
    )


def tap_source(tap):
    a, b = divmod(tap, 3)
    plane = (a % 2) * 2 + b % 2
    return plane, (a == 2) * S + (b == 2)


def front(full, xp, hid, sl1, bdt, h2, sl2):
    weight = full[:, :, :, 0:256].reshape(512, 256)
    for k in range(4):
        hid[k, 10 * S :] = jnp.zeros((PLANE - 10 * S, 512), F32)
        pixels = xp[k].astype(BF)
        for n in range(2):
            half = slice(256 * n, 256 * n + 256)
            pre = mm(pixels, weight[half], NT)
            gate = sigmoid(pre)
            act = pre * gate
            hid[k, : 10 * S, half] = act.astype(BF).astype(F32)
            sl1[k, : 10 * S, half] = gate + act * (1.0 - gate)

    lane = lax.broadcasted_iota(jnp.int32, (16, 128), 1) // GW
    for tap in range(9):
        first = 256 + 128 * (tap // 8)
        for u in range(4):
            t, v = divmod(u, 2)
            for g in range(8):
                at = divmod(8 * u + g, NY)
                piece = full[at[0], at[1], :, first : first + 128].astype(F32)
                turn = ((g - tap % 8) * 16) % 128
                if turn:
                    piece = pltpu.roll(piece, turn, 1)
                piece = jnp.where(lane == g, piece, 0.0).astype(BF)
                low = v * 128 + g * 16
                bdt[tap, t, low : low + 16, v * 128 : v * 128 + 128] = piece

    for t in range(2):
        half = slice(256 * t, 256 * t + 256)
        pre = jnp.zeros((MO, 256), F32)
        for tap in range(9):
            k, off = tap_source(tap)
            pre = pre + mm(hid[k, off : off + MO, half].astype(BF), bdt[tap, t], NT)
        gate = sigmoid(pre)
        act = pre * gate
        h2[:, half] = act.astype(BF)
        sl2[:, half] = gate + act * (1.0 - gate)


def whole_kernel(
    nr, nc, w_reduce, w_group, w_expand, w_short, region, cot,
    block_out, region_grad, out,
    full, xp, c32, hid, sl1, bdt, h2, sl2, wt, wg, regv, cotv, image, lstrip, fstrip, top, bot, cbot, lft, rgt,
    g2o, gs, gso, g2, g1, rg, gt, rc, send, land, s2, rz, rx,
    ls, zs, zr, us, ur, ds, dr_, fs, fr, cs, cr, hs, hr,
    rcs, rcr, rys, ryr, rzs, rzr, rxs, rxr,
):
    nz, nx, nh = nc // NY, nr // 2, nc // NY // 2
    row, col = lax.axis_index("row"), lax.axis_index("col")
    x, core = row // 2, lax.rem(row, 2)
    partner = row + 1 - 2 * core
    z, y = col // NY, lax.rem(col, NY)
    y_up, y_down, y_far = lax.rem(y + 1, NY), lax.rem(y + NY - 1, NY), lax.rem(y + 2, NY)
    lanes = pl.ds(pl.multiple_of(core * HALF, 128), HALF)
    has_up, has_down = row > 0, row < nr - 1
    has_left, has_right = col > 0, col < nc - 1

    barrier = pltpu.get_barrier_semaphore()

    def greet(to_row, to_col):
        pl.semaphore_signal(barrier, inc=1, device_id=(to_row, to_col), device_id_type=MESH)

    for d in range(1, nz):
        greet(row, lax.rem(z + d, nz) * NY + y)
    greet(row, z * NY + y_up)
    greet(row, z * NY + y_down)
    greet(row, z * NY + y_far)
    greet(partner, col)
    for d in range(1, nx):
        greet(2 * lax.rem(x + d, nx), col)
        greet(2 * lax.rem(x + d, nx) + 1, col)
    count = nz + 3 + 2 * (nx - 1)
    for dr in (-1, 0, 1):
        for dc in (-1, 0, 1):
            if dr == 0 and dc == 0:
                continue
            there = None
            for step, less, more in ((dr, has_up, has_down), (dc, has_left, has_right)):
                if step:
                    flag = more if step > 0 else less
                    there = flag if there is None else there & flag
            count = count + there.astype(jnp.int32)

            @pl.when(there)
            def _(dr=dr, dc=dc):
                greet(row + dr, col + dc)

    loads = [
        pltpu.make_async_copy(region, regv, ls.at[0]),
        pltpu.make_async_copy(cot, cotv, ls.at[1]),
        pltpu.make_async_copy(w_reduce, wt.at[:, 0:256], ls.at[2]),
        pltpu.make_async_copy(w_short, wt.at[:, 512:768], ls.at[3]),
        pltpu.make_async_copy(w_expand, wt.at[:, 768:1280], ls.at[4]),
        pltpu.make_async_copy(w_group, wg, ls.at[5]),
    ]
    for load in loads:
        load.start()
    wt[:, 256:512] = jnp.zeros((wt.shape[0], 256), BF)
    image[...] = jnp.zeros_like(image)
    bdt[...] = jnp.zeros_like(bdt)
    c32[...] = jnp.zeros_like(c32)

    lpart = (pl.ds(8, 8), pl.ds(0, 16), pl.ds(0, 8))
    fpart = (pl.ds(0, 1), pl.ds(0, 3), pl.ds(1, 2))
    plan = [
        (has_down, 1, 0, regv.at[15], top, 0),
        (has_up, -1, 0, regv.at[pl.ds(0, 2)], bot, 1),
        (has_up, -1, 0, cotv.at[0], cbot, 2),
    ]
    for k, (there, step) in enumerate(((has_down, 1), (None, 0), (has_up, -1))):
        right = has_right if there is None else has_right & there
        left = has_left if there is None else has_left & there
        plan.append((right, step, 1, lstrip.at[lpart[k]], lft.at[k, lpart[k]], 3 + k))
        plan.append((left, step, -1, fstrip.at[fpart[k]], rgt.at[k, fpart[k]], 6 + k))
    above = {0: has_up, 1: has_down, 2: has_down}
    for k, there in enumerate((has_up, None, has_down)):
        above[3 + k] = has_left if there is None else has_left & there
        above[6 + k] = has_right if there is None else has_right & there
    zero_of = {0: top, 1: bot, 2: cbot}
    for k in range(3):
        zero_of[3 + k] = lft.at[k]
        zero_of[6 + k] = rgt.at[k]
    for n, ref in zero_of.items():

        @pl.when(jnp.logical_not(above[n]))
        def _(ref=ref):
            ref[...] = jnp.zeros(ref.shape, ref.dtype)

    for load in loads:
        load.wait()
    wt[:, 256:400] = wg[...]
    full[z, y, :, lanes] = wt[:, lanes]
    for h in range(2):
        side = slice(128 * h, 128 * h + 128)
        for r in range(16):
            image[h, (r + 1) * PW + 1 : (r + 1) * PW + 33] = regv[r, :, side].astype(F32)
        lstrip[:, side] = image[h, pl.ds(PW + 32, 16, stride=PW), :].astype(BF)
        for q in range(2):
            for e in range(2):
                fstrip[1 - e, :, 256 * q + 128 * h : 256 * q + 128 * h + 128] = image[
                    h, pl.ds((8 * e + 1) * PW + 1 + q, 8, stride=PW), :
                ].astype(BF)
    for h in range(4):
        side = slice(128 * h, 128 * h + 128)
        for i in range(8):
            c32[h, i * S : i * S + 16] = cotv[i, :, side].astype(F32)
        fstrip[2, :, side] = c32[h, pl.ds(0, 8, stride=S), :].astype(BF)

    pl.semaphore_wait(barrier, count)

    order = [nz // 2] + [n for d in range(nz // 2 - 1, 0, -1) for n in (d, nz - d)]
    across_x = [nx // 2] + [n for d in range(nx // 2 - 1, 0, -1) for n in (d, nx - d)]
    late = order[:3]
    relayed = [d for d in [0] + order[::-1] if d not in late]
    along_z, upward, downward, forward = {}, {}, {}, {}
    for d in order[::-1]:
        copy = remote(
            wt.at[:, lanes], full.at[z, y, :, lanes], zs.at[d], zr.at[d],
            row, lax.rem(z + d, nz) * NY + y,
        )
        copy.start()
        along_z[d] = copy

    def to_neighbours(d):
        here = full.at[lax.rem(z + nz - d, nz), y, :, lanes]
        upward[d] = remote(here, here, us.at[d], ur.at[d], row, z * NY + y_up)
        downward[d] = remote(here, here, ds.at[d], dr_.at[d], row, z * NY + y_down)
        if d in late:
            forward[d] = remote(here, here, fs.at[d], fr.at[d], row, z * NY + y_far)
            forward[d].start()
        upward[d].start()
        downward[d].start()

    to_neighbours(0)
    halos = []
    for there, dr, dc, src, dst, n in plan:
        copy = remote(src, dst, hs.at[n], hr.at[n], row + dr, col + dc)
        halos.append((there, copy, n))

        @pl.when(there)
        def _(copy=copy):
            copy.start()

    nearest = [0] + order[::-1]
    for d in nearest[1:]:
        along_z[d].wait_recv()
        to_neighbours(d)

    columns = []

    def column(at):
        block = full.at[:, at, :, lanes]
        n = len(columns)
        copy = remote(block, block, cs.at[n], cr.at[n], partner, col)
        copy.start()
        columns.append(copy)

    column(y)

    for d in nearest:
        b = lax.rem(z + nz - d, nz)
        upward[d].wait_recv()
        if d in relayed[::2]:
            here = full.at[b, y_down, :, lanes]
            forward[d] = remote(here, here, fs.at[d], fr.at[d], row, z * NY + y_up)
            forward[d].start()
        downward[d].wait_recv()
        if d in relayed[1::2]:
            here = full.at[b, y_up, :, lanes]
            forward[d] = remote(here, here, fs.at[d], fr.at[d], row, z * NY + y_down)
            forward[d].start()
    column(y_up)
    column(y_down)

    for there, copy, n in halos:

        @pl.when(above[n])
        def _(copy=copy):
            copy.wait_recv()

    for h in range(2):
        side = slice(128 * h, 128 * h + 128)
        image[h, 1:33] = top[:, side].astype(F32)
        for r in range(2):
            image[h, (17 + r) * PW + 1 : (17 + r) * PW + 33] = bot[r, :, side].astype(F32)
        image[h, pl.ds(PW, 16, stride=PW), :] = lft[1, :, side].astype(F32)
        image[h, 0:1] = lft[0, 8:16, side].astype(F32)[7:8]
        below = lft[2, 0:8, side].astype(F32)
        for r in range(2):
            image[h, (17 + r) * PW : (17 + r) * PW + 1] = below[r : r + 1]
        for q in range(2):
            side = slice(256 * q + 128 * h, 256 * q + 128 * h + 128)
            for e in range(2):
                low = (8 * e + 1) * PW + 33 + q
                image[h, pl.ds(low, 8, stride=PW), :] = rgt[1, 1 - e, :, side].astype(F32)
            image[h, 33 + q : 34 + q] = rgt[0, 0, :, side].astype(F32)[7:8]
            corner = rgt[2, 1, :, side].astype(F32)
            for r in range(2):
                low = (17 + r) * PW + 33 + q
                image[h, low : low + 1] = corner[r : r + 1]
    for h in range(4):
        side = slice(128 * h, 128 * h + 128)
        c32[h, 8 * S : 8 * S + 16] = cbot[:, side].astype(F32)
        c32[h, pl.ds(16, 8, stride=S), :] = rgt[1, 2, :, side].astype(F32)
        c32[h, 8 * S + 16 : 8 * S + 17] = rgt[2, 2, :, side].astype(F32)[0:1]
    for k in range(4):
        pr, pc = divmod(k, 2)
        for i in range(10):
            for h in range(2):
                xp[k, i * S : (i + 1) * S, 128 * h : 128 * h + 128] = image[
                    h, pl.ds((2 * i + pr) * PW + pc, S, stride=2), :
                ]

    for d in nearest:
        forward[d].wait_recv()
    column(y_far)
    for copy in columns:
        copy.wait_recv()

    front(full, xp, hid, sl1, bdt, h2, sl2)
    w_r = full[:, :, :, 0:256].reshape(512, 256)
    w_s = full[:, :, :, 512:768].reshape(512, 256)
    w_e = full[:, :, :, 768:1280].reshape(512, 512)
    mine = [pl.ds(pl.multiple_of(first + core * wide, 128), wide) for first, wide in CHUNKS]
    other = [pl.ds(pl.multiple_of(first + (1 - core) * wide, 128), wide) for first, wide in CHUNKS]
    chunks = (1, 0)

    across, along_y, turn_z, along_x = {}, {}, {}, {}

    def start_across(q):
        for n, at in enumerate((y_far, y_up, y_down, y)):
            copy = remote(
                gt.at[:, at, :, other[q]], rc.at[:, at, :, LOCAL[q]],
                rcs.at[q, n], rcr.at[q, n], partner, col,
            )
            copy.start()
            across[q, n] = copy

    def chip(q, n, at):
        return gt[n, at, :, mine[q]].astype(F32) + rc[n, at, :, LOCAL[q]].astype(F32)

    def start_y(q, n, to):
        copy = remote(
            send.at[n, :, :, LOCAL[q]], land.at[n, :, :, LOCAL[q]],
            rys.at[q, n], ryr.at[q, n], row, z * NY + to,
        )
        copy.start()
        along_y[q, n] = copy

    def fill(q, n, low, at, extra=None):
        for k in range(nh):
            term = chip(q, low + k, at)
            if extra is not None:
                term = term + land[extra, k, :, LOCAL[q]].astype(F32)
            send[n, k, :, LOCAL[q]] = term.astype(BF)

    def y_first(q):
        across[q, 0].wait_recv()
        fill(q, 0, 0, y_far)
        start_y(q, 0, y_up)
        fill(q, 1, nh, y_far)
        start_y(q, 1, y_down)
        across[q, 1].wait_recv()
        fill(q, 2, nh, y_up)
        start_y(q, 2, y_up)
        across[q, 2].wait_recv()
        fill(q, 3, 0, y_down)
        start_y(q, 3, y_down)

    def y_second(q):
        along_y[q, 0].wait_recv()
        fill(q, 4, 0, y_up, 0)
        start_y(q, 4, y_up)
        along_y[q, 1].wait_recv()
        fill(q, 5, nh, y_down, 1)
        start_y(q, 5, y_down)

    def put(first, lanes, value):
        blocks = value.reshape(value.shape[0] // (NY * GW), NY, GW, value.shape[1])
        gt[pl.ds(first // (NY * GW), blocks.shape[0]), :, :, lanes] = blocks.astype(BF)

    own = lax.rem(lax.broadcasted_iota(jnp.int32, (MW, 256), 0), S) < 16
    strided = xp[3, :MO].astype(BF)
    for n in range(2):
        half = slice(256 * n, 256 * n + 256)
        total = mm(h2[...], w_e[half], NT) + mm(strided, w_s[half], NT)
        gate = sigmoid(total)
        act = total * gate
        for i in range(8):
            block_out[i, :, half] = act[i * S : i * S + 16].astype(BF)
        cots = jnp.concatenate([c32[2 * n], c32[2 * n + 1]], axis=1)
        grad = cots * (gate + act * (1.0 - gate))
        gs[:, half] = grad.astype(BF)
        gso[:, half] = jnp.where(own, grad[:MW], 0.0).astype(BF)

    for n in range(2):
        half = slice(256 * n, 256 * n + 256)
        put(256 * n, slice(512, 768), mm(gso[:, half], strided[:MW], TN))
        for m in range(2):
            cols = slice(256 * m, 256 * m + 256)
            put(256 * n, slice(768 + 256 * m, 1024 + 256 * m), mm(gso[:, half], h2[:MW, cols], TN))
    start_across(1)

    for t in range(2):
        half = slice(256 * t, 256 * t + 256)
        grad = mm(gs[...], w_e[:, 256 * t : 256 * t + 256], NN) * sl2[:, half]
        g2[:, half] = grad.astype(BF).astype(F32)
        g2o[:, half] = jnp.where(own, grad[:MW], 0.0).astype(BF)

    lane = lax.broadcasted_iota(jnp.int32, (16, 128), 1) // GW
    for u in range(4):
        block = slice(128 * u, 128 * u + 128)
        sums = [[jnp.zeros((16, 128), F32)] * 8, [jnp.zeros((16, 128), F32)] * 8]
        for tap in range(9):
            k, off = tap_source(tap)
            outer = mm(g2o[:, block], hid[k, off : off + MW, block].astype(BF), TN)
            for g in range(8):
                piece = outer[g * 16 : g * 16 + 16]
                turn = ((tap % 8 - g) * 16) % 128
                if turn:
                    piece = pltpu.roll(piece, turn, 1)
                sums[tap // 8][g] = jnp.where(lane == tap % 8, piece, sums[tap // 8][g])
        for h in range(2):
            for g in range(8):
                at = divmod(8 * u + g, NY)
                gt[at[0], at[1], :, 256 + 128 * h : 384 + 128 * h] = sums[h][g].astype(BF)


    y_first(1)

    for k in range(4):
        pr, pc = divmod(k, 2)
        window = (1 - pr) * S + (1 - pc)
        for t in range(2):
            half = slice(256 * t, 256 * t + 256)
            spread = jnp.zeros((MW, 256), F32)
            for tap in range(9):
                a, b = divmod(tap, 3)
                if tap_source(tap)[0] != k:
                    continue
                off = (a == 0) * S + (b == 0)
                spread = spread + mm(g2[off : off + MW, half].astype(BF), bdt[tap, t], NN)
            grad = jnp.where(own, spread * sl1[k, window : window + MW, half], 0.0)
            g1[k, :, half] = grad.astype(BF)
    for n in range(2):
        half = slice(256 * n, 256 * n + 256)
        grad = jnp.zeros((256, 256), F32)
        for k in range(4):
            pr, pc = divmod(k, 2)
            window = (1 - pr) * S + (1 - pc)
            grad = grad + mm(g1[k, :, half], xp[k, window : window + MW].astype(BF), TN)
        put(256 * n, slice(0, 256), grad)
    start_across(0)

    for k in range(4):
        pr, pc = divmod(k, 2)
        back = mm(g1[k], w_r, NN)
        if k == 3:
            back = back + mm(gso[...], w_s, NN)
        for i in range(8):
            line = (2 * i + 1 - pr) * 32 + 1 - pc
            for h in range(2):
                rg[h, pl.ds(line, 16, stride=2), :] = back[
                    i * S : i * S + 16, 128 * h : 128 * h + 128
                ]
    y_first(0)
    y_second(1)
    for r in range(16):
        for h in range(2):
            region_grad[r, :, 128 * h : 128 * h + 128] = rg[h, 32 * r : 32 * r + 32].astype(BF)
    y_second(0)

    for q in chunks:
        part = LOCAL[q]
        across[q, 3].wait_recv()
        for n in (2, 3, 4, 5):
            along_y[q, n].wait_recv()
        for k in range(nh):
            s2[k, :, part] = (
                chip(q, k, y) + land[3, k, :, part].astype(F32) + land[4, k, :, part].astype(F32)
            )
            s2[nh + k, :, part] = (
                chip(q, nh + k, y) + land[2, k, :, part].astype(F32) + land[5, k, :, part].astype(F32)
            )
        for d in order[::-1]:
            to = lax.rem(z + d, nz)
            rz[0, d, :, part] = s2[to, :, part].astype(BF)
            copy = remote(
                rz.at[0, d, :, part], rz.at[1, d, :, part], rzs.at[q, d], rzr.at[q, d], row, to * NY + y
            )
            copy.start()
            turn_z[q, d] = copy
    for q in chunks:
        part = LOCAL[q]
        term = s2[z, :, part]
        for d in range(1, nz):
            turn_z[q, d].wait_recv()
            term = term + rz[1, d, :, part].astype(F32)
        rx[x, :, mine[q]] = term.astype(BF)
        for d in across_x:
            for e in range(2):
                here = rx.at[x, :, mine[q]]
                to = lax.rem(core + e, 2)
                copy = remote(
                    here, here, rxs.at[q, 2 * d + e], rxr.at[q, 2 * d + e],
                    2 * lax.rem(x + d, nx) + to, col,
                )
                copy.start()
                along_x[q, 2 * d + e] = copy
        here = rx.at[x, :, mine[q]]
        copy = remote(here, here, rxs.at[q, 1], rxr.at[q, 1], partner, col)
        copy.start()
        along_x[q, 1] = copy
    for copy in along_x.values():
        copy.wait_recv()
    term = rx[0].astype(F32)
    for n in range(1, nx):
        term = term + rx[n].astype(F32)
    out[...] = term
    for there, copy, n in halos:

        @pl.when(there)
        def _(copy=copy):
            copy.wait_send()

    for copy in columns:
        copy.wait_send()
    for group in (along_z, upward, downward, forward, across, along_y, turn_z, along_x):
        for copy in group.values():
            copy.wait_send()


def whole(nr, nc, *arrays):
    nz, nx = nc // NY, nr // 2
    kw = GW
    shape = jax.ShapeDtypeStruct
    hbm = pl.BlockSpec(memory_space=pltpu.HBM)
    dma = pltpu.SemaphoreType.DMA
    return pl.pallas_call(
        functools.partial(whole_kernel, nr, nc),
        out_shape=(
            shape((8, 16, 512), BF),
            shape((16, 32, 256), BF),
            shape((kw, LANES), F32),
        ),
        in_specs=[hbm] * 6,
        out_specs=(VMEM,) * 3,
        scratch_shapes=[
            pltpu.VMEM((nz, NY, kw, LANES), BF),
            pltpu.VMEM((4, 10 * S, 256), F32),
            pltpu.VMEM((4, MO, 128), F32),
            pltpu.VMEM((4, PLANE, 512), F32),
            pltpu.VMEM((4, PLANE, 512), F32),
            pltpu.VMEM((9, 2, 256, 256), BF),
            pltpu.VMEM((MO, 512), BF),
            pltpu.VMEM((MO, 512), F32),
            pltpu.VMEM((kw, LANES), BF),
            pltpu.VMEM((kw, 144), BF),
            pltpu.VMEM((16, 32, 256), BF),
            pltpu.VMEM((8, 16, 512), BF),
            pltpu.VMEM((2, 20 * PW, 128), F32),
            pltpu.VMEM((16, 256), BF),
            pltpu.VMEM((3, 8, 512), BF),
            pltpu.VMEM((32, 256), BF),
            pltpu.VMEM((2, 32, 256), BF),
            pltpu.VMEM((16, 512), BF),
            pltpu.VMEM((3, 16, 256), BF),
            pltpu.VMEM((3, 3, 8, 512), BF),
            pltpu.VMEM((MW, 512), BF),
            pltpu.VMEM((MO, 512), BF),
            pltpu.VMEM((MW, 512), BF),
            pltpu.VMEM((MO, 512), F32),
            pltpu.VMEM((4, MW, 512), BF),
            pltpu.VMEM((2, 512, 128), F32),
            pltpu.VMEM((nz, NY, kw, LANES), BF),
            pltpu.VMEM((nz, NY, kw, HALF), BF),
            pltpu.VMEM((6, nz // 2, kw, HALF), BF),
            pltpu.VMEM((6, nz // 2, kw, HALF), BF),
            pltpu.VMEM((nz, kw, HALF), F32),
            pltpu.VMEM((2, nz, kw, HALF), BF),
            pltpu.VMEM((nx, kw, LANES), BF),
            dma((6,)),
            dma((nz,)), dma((nz,)), dma((nz,)), dma((nz,)),
            dma((nz,)), dma((nz,)), dma((nz,)), dma((nz,)),
            dma((4,)), dma((4,)), dma((9,)), dma((9,)),
            dma((2, 4)), dma((2, 4)), dma((2, 6)), dma((2, 6)),
            dma((2, nz)), dma((2, nz)), dma((2, nr)), dma((2, nr)),
        ],
        compiler_params=pltpu.CompilerParams(
            collective_id=0, has_side_effects=True, vmem_limit_bytes=48 << 20
        ),
        name="whole",
    )(*(pltpu.with_memory_space_constraint(a, pltpu.HBM) for a in arrays))


def store_kernel(
    block_out, region_grad, slab,
    block_to, region_to, reduce_grad, group_grad, expand_grad, shortcut_grad, group, sems,
):
    pairs = [
        (region_grad, region_to),
        (block_out, block_to),
        (slab.at[:, 768:1280], expand_grad),
        (slab.at[:, 0:256], reduce_grad),
        (slab.at[:, 512:768], shortcut_grad),
        (group, group_grad),
    ]
    copies = [pltpu.make_async_copy(a, b, sems.at[n]) for n, (a, b) in enumerate(pairs)]
    for copy in copies[:-1]:
        copy.start()
    group[...] = slab[:, 256:400]
    copies[-1].start()
    for copy in copies:
        copy.wait()


def store(block_out, region_grad, slab):
    kw = slab.shape[0]
    shape = jax.ShapeDtypeStruct
    return pl.pallas_call(
        store_kernel,
        out_shape=(
            shape(block_out.shape, BF),
            shape(region_grad.shape, BF),
            *(shape((kw, n), F32) for n in (256, 144, 512, 256)),
        ),
        in_specs=[VMEM] * 3,
        out_specs=(pl.BlockSpec(memory_space=pltpu.HBM),) * 6,
        scratch_shapes=[pltpu.VMEM((kw, 144), F32), pltpu.SemaphoreType.DMA((6,))],
        compiler_params=pltpu.CompilerParams(vmem_limit_bytes=4 << 20),
        name="store",
    )(block_out, region_grad, slab)


def solution(mesh):
    nr, nc = mesh.shape["row"], mesh.shape["col"]

    def per_device(region, reduce_weight, group_weight, expand_weight, shortcut_weight, cotangent):
        block_out, region_grad, *grads = store(
            *whole(
                nr, nc, reduce_weight.T, group_weight.T, expand_weight.T, shortcut_weight.T,
                region, cotangent,
            )
        )
        return (block_out, region_grad, *(grad.T for grad in grads))

    weight = P(None, "col")
    tile = P("row", "col", None)
    return jax.shard_map(
        per_device,
        mesh=mesh,
        in_specs=(tile, weight, weight, weight, weight, tile),
        out_specs=(tile, tile, weight, weight, weight, weight),
        check_vma=False,
    )
```
